256 devices in a mesh: frame: 32 (over z_hi, y, x), head: 8 (over z_lo, core).
Axes of the slice: x: 4, y: 4, z: 8 (z_hi: 2, z_lo: 4; z = z_hi * 4 + z_lo), core: 2. Of those that a mesh axis runs over, the one named last changes fastest.
Arguments:
- queries: bfloat16 [8192, 5120], P('frame', 'head'), may hold values from -12 to 12
- keys: bfloat16 [8192, 5120], P('frame', 'head'), may hold values from -12 to 12
- values: bfloat16 [8192, 5120], P('frame', 'head'), may hold values from -6 to 6
- policy_grad: bfloat16 [8192, 5120], P('frame', 'head'), may hold values from -6 to 6
- ref_velocity: bfloat16 [8192, 5120], P('frame', 'head'), may hold values from -6 to 6
- key_lists: int32 [64, 6], P('frame'), may hold values from 0 to 63, as said below
- frame_tokens: int32 [64], replicated, may hold values from 32 to 128, as said below
Outputs:
- grad_queries: bfloat16 [8192, 5120], P('frame', 'head')
- grad_keys: bfloat16 [8192, 5120], P('frame', 'head')
- grad_values: bfloat16 [8192, 5120], P('frame', 'head')
The draws below stay inside these ranges and needn't reach their ends.
Inputs may be any that keep to these rules, and one draw needn't show every extreme that they name: `key_lists`: row b holds 6 distinct blocks: b, the next block of the same index of frame (cyclic over its 2 blocks), and four blocks on indices of frame that differ from b's index by distinct signed powers of two. `frame_tokens`: some block is full.
All inputs are finite; a program needn't handle non-finite values.
Results may differ from the reference program's by a relative error of at most 0.011.
Values may be sent and summed in bfloat16 or wider, within the bound.
No kernel may reach another device: no remote copies, remote signals or barrier semaphores. Data moves between devices by JAX's collectives and lax.ppermute only.
A program may use at most 128 MiB of HBM per device.

```python
import math
import jax
import jax.numpy as jnp
from jax import lax

HEADS = 40
HD = 128
BLK = 128
KLIST = 6
TOKENS = 8192
FBLK = 2
NBLK = 64
SHARDS = 32
LEVELS = 5


def draw_queries(key, part):
    shape = (TOKENS, HEADS * HD)
    base = jax.random.normal(jax.random.fold_in(key, 1), shape, jnp.float32)
    return base.astype(jnp.bfloat16)


def draw_keys(key, part):
    shape = (TOKENS, HEADS * HD)
    base = jax.random.normal(jax.random.fold_in(key, 2), shape, jnp.float32)
    return base.astype(jnp.bfloat16)


def draw_frame_tokens(key, part):
    counts = jax.random.randint(jax.random.fold_in(key, 3), (NBLK,), BLK // 4, BLK + 1, jnp.int32)
    counts = counts.at[0].set(BLK)
    return counts.at[1].set(BLK // 4)


def draw_key_lists(key, part):
    blocks = jnp.arange(NBLK, dtype=jnp.int32)
    device = blocks // FBLK
    place = blocks % FBLK
    first = blocks
    second = device * FBLK + (place + 1) % FBLK
    steps = []
    for level in range(LEVELS):
        steps.append(1 << level)
        steps.append(-(1 << level))
    steps = jnp.array(steps, dtype=jnp.int32)
    target = device[:, None] + steps[None, :]
    inside = (target >= 0) & (target < SHARDS)
    scores = jax.random.randint(jax.random.fold_in(key, 4), (NBLK, 2 * LEVELS), 0, 1 << 16, jnp.int32) * 64 + jnp.arange(2 * LEVELS, dtype=jnp.int32)[None, :]
    scores = jnp.where(inside, scores, -1)
    picked = jax.lax.top_k(scores, 4)[1]
    chosen = jnp.take_along_axis(target, picked, axis=1)
    within = jax.random.randint(jax.random.fold_in(key, 5), (NBLK, 4), 0, FBLK, jnp.int32)
    far_blocks = chosen * FBLK + within
    return jnp.concatenate([first[:, None], second[:, None], far_blocks], axis=1).astype(jnp.int32)


def level_of(key, shape, cuts, smallest, largest):
    gain, own = 1.0, jax.random.fold_in(key, 6)
    for dim, blocks in cuts:
        steps = jnp.exp(jax.random.uniform(jax.random.fold_in(own, dim), (blocks,), jnp.float32, smallest / len(cuts), largest / len(cuts)))
        gain = gain * jnp.repeat(steps, shape[dim] // blocks).reshape([-1 if axis == dim else 1 for axis in range(len(shape))])
    return gain


def normal_values(key, extent, width, bound, split=(), kind=jnp.bfloat16):
    result = width * jax.random.normal(key, extent, jnp.float32)
    if split:
        result = result * level_of(key, extent, split, -0.22, 0.18)
    return jnp.clip(result, -bound, bound).astype(kind)


def setup_inputs(seed: int = 0) -> dict:
    splits = jax.random.split(jax.random.key(seed), 8)
    return {
        "queries": draw_queries(jax.random.fold_in(splits[7], 71), 0),
        "keys": draw_keys(jax.random.fold_in(splits[7], 71), 0),
        "values": normal_values(splits[2], (TOKENS, HEADS * HD), 1.0, 6.0, ((0, 32), (1, 8))),
        "policy_grad": normal_values(splits[3], (TOKENS, HEADS * HD), 1.0, 6.0, ((0, 32), (1, 8))),
        "ref_velocity": normal_values(splits[4], (TOKENS, HEADS * HD), 1.0, 6.0, ((0, 32), (1, 8))),
        "key_lists": draw_key_lists(jax.random.fold_in(splits[7], 71), 0),
        "frame_tokens": draw_frame_tokens(jax.random.fold_in(splits[7], 71), 0),
    }


kl_weight = 1.0

def block_forward(query_block, key_block, value_block, valid, scale):
    scores = jnp.einsum('qhd,khd->hqk', query_block.astype(jnp.float32), key_block.astype(jnp.float32), precision=lax.Precision.HIGHEST) * scale
    scores = jnp.where(valid[None, None, :], scores, -1e+30)
    highest = lax.optimization_barrier(jnp.max(scores, axis=-1, keepdims=True))
    expd = jnp.exp(scores - highest)
    probs = expd / lax.optimization_barrier(jnp.sum(expd, axis=-1, keepdims=True))
    probs16 = probs.astype(jnp.bfloat16)
    attn = jnp.einsum('hqk,khd->qhd', probs16.astype(jnp.float32), value_block.astype(jnp.float32), precision=lax.Precision.HIGHEST)
    return (probs, probs16, attn)

def reference(queries, keys, values, policy_grad, ref_velocity, key_lists, frame_tokens):
    scale = 1.0 / math.sqrt(HD)
    query4 = queries.reshape(NBLK, BLK, HEADS, HD)
    key4 = keys.reshape(NBLK, BLK, HEADS, HD)
    value4 = values.reshape(NBLK, BLK, HEADS, HD)

    def fetch(ids):
        key_block = key4[ids].reshape(KLIST * BLK, HEADS, HD)
        value_block = value4[ids].reshape(KLIST * BLK, HEADS, HD)
        valid = (jnp.arange(BLK, dtype=jnp.int32)[None, :] < frame_tokens[ids][:, None]).reshape(-1)
        return (key_block, value_block, valid)

    def forward_one(index):
        key_block, value_block, valid = fetch(key_lists[index])
        return block_forward(query4[index], key_block, value_block, valid, scale)[2]
    attn_all = lax.map(forward_one, jnp.arange(NBLK, dtype=jnp.int32))
    diff = attn_all - ref_velocity.reshape(NBLK, BLK, HEADS, HD).astype(jnp.float32)
    kl = lax.optimization_barrier(jnp.sum(diff * diff, axis=(2, 3))) / (HEADS * HD)
    grad_attn = policy_grad.reshape(NBLK, BLK, HEADS, HD).astype(jnp.float32) + kl_weight * diff / (1.0 + kl)[:, :, None, None]
    grad16 = grad_attn.astype(jnp.bfloat16)

    def backward_one(index):
        key_block, value_block, valid = fetch(key_lists[index])
        probs, probs16, attn = block_forward(query4[index], key_block, value_block, valid, scale)
        upstream = grad16[index].astype(jnp.float32)
        grad_probs = jnp.einsum('qhd,khd->hqk', upstream, value_block.astype(jnp.float32), precision=lax.Precision.HIGHEST)
        delta = lax.optimization_barrier(jnp.sum(upstream * attn, axis=-1)).T
        grad_scores16 = (probs * (grad_probs - delta[:, :, None])).astype(jnp.bfloat16).astype(jnp.float32)
        grad_q = (jnp.einsum('hqk,khd->qhd', grad_scores16, key_block.astype(jnp.float32), precision=lax.Precision.HIGHEST) * scale).astype(jnp.bfloat16)
        part_k = jnp.einsum('hqk,qhd->khd', grad_scores16, query4[index].astype(jnp.float32), precision=lax.Precision.HIGHEST) * scale
        part_v = jnp.einsum('hqk,qhd->khd', probs16.astype(jnp.float32), upstream, precision=lax.Precision.HIGHEST)
        return (grad_q, part_k.reshape(KLIST, BLK * HEADS * HD), part_v.reshape(KLIST, BLK * HEADS * HD))

    def device_step(carry, device):
        acc_k, acc_v = carry
        blocks = device * FBLK + jnp.arange(FBLK, dtype=jnp.int32)
        grad_q, part_k, part_v = lax.map(backward_one, blocks)
        ids = key_lists[blocks].reshape(-1).astype(jnp.int32)
        same = (ids[:, None] == ids[None, :]).astype(jnp.float32)
        earlier = lax.optimization_barrier(jnp.sum(jnp.tril(same, -1), axis=1))
        first = (earlier == 0.0)[:, None]
        remote = (ids // FBLK != device)[:, None]
        part_k = jnp.dot(same, part_k.reshape(FBLK * KLIST, -1), precision=lax.Precision.HIGHEST)
        part_v = jnp.dot(same, part_v.reshape(FBLK * KLIST, -1), precision=lax.Precision.HIGHEST)
        round_k = lax.optimization_barrier(part_k.astype(jnp.bfloat16)).astype(jnp.float32)
        round_v = lax.optimization_barrier(part_v.astype(jnp.bfloat16)).astype(jnp.float32)
        part_k = jnp.where(remote, round_k, part_k)
        part_v = jnp.where(remote, round_v, part_v)
        acc_k = acc_k.at[ids].add(jnp.where(first, part_k, jnp.float32(0.0)))
        acc_v = acc_v.at[ids].add(jnp.where(first, part_v, jnp.float32(0.0)))
        return ((acc_k, acc_v), grad_q)
    zeros = jnp.zeros((NBLK, BLK * HEADS * HD), jnp.float32)
    (acc_k, acc_v), grad_q = lax.scan(device_step, (zeros, zeros), jnp.arange(SHARDS, dtype=jnp.int32))
    grad_queries = grad_q.reshape(TOKENS, HEADS * HD)
    grad_keys = acc_k.reshape(TOKENS, HEADS * HD).astype(jnp.bfloat16)
    grad_values = acc_v.reshape(TOKENS, HEADS * HD).astype(jnp.bfloat16)
    return (grad_queries, grad_keys, grad_values)
```

```python
import functools
import math

import jax
import jax.numpy as jnp
import numpy as np
from jax import lax
from jax.experimental import pallas as pl
from jax.experimental.pallas import tpu as pltpu
from jax.sharding import PartitionSpec as P

HEADS = 40
HD = 128
BLK = 128
TAIL = 16

kl_weight = 1.0


WIDE = 2

NT = (((1,), (1,)), ((), ()))
NN = (((1,), (0,)), ((), ()))


def matmul(left, right, dims):
    return lax.dot_general(left, right, dims, preferred_element_type=jnp.float32)


def diagonal():
    return lax.broadcasted_iota(jnp.int32, (BLK, BLK), 0) == lax.broadcasted_iota(
        jnp.int32, (BLK, BLK), 1
    )


def as_row(column, eye):
    return jnp.sum(jnp.where(eye, column, 0.0), axis=0, keepdims=True)


def as_column(row, eye):
    return jnp.sum(jnp.where(eye, row, 0.0), axis=1, keepdims=True)


def bring(sources, targets, sems, first, start):
    for position, (source, target) in enumerate(zip(sources, targets)):
        copy = pltpu.make_async_copy(source, target, sems.at[first + position])
        if start:
            copy.start()
        else:
            copy.wait()


def fetch(sources, pool, sems, used, start):
    height = pool.shape[0] // len(sources)
    for position, source in enumerate(sources):

        @pl.when(used[position] != 0)
        def _():
            copy = pltpu.make_async_copy(
                source, pool.at[pl.ds(position * height, height)], sems.at[position]
            )
            if start:
                copy.start()
            else:
                copy.wait()


def listed(pool, slots, block, list_len, cols):
    return jnp.concatenate(
        [
            pool[pl.ds(pl.multiple_of(slots[block * list_len + s] * BLK, BLK), BLK), cols]
            for s in range(list_len)
        ],
        axis=0,
    )


def block_probs(query, key_block, counts, block, list_len, scale):
    scores = matmul(query, key_block, NT) * scale
    lane = lax.broadcasted_iota(jnp.int32, (BLK, BLK), 1)
    scores = jnp.concatenate(
        [
            jnp.where(
                lane < counts[block * list_len + s], scores[:, s * BLK : (s + 1) * BLK], -1e30
            )
            for s in range(list_len)
        ],
        axis=1,
    )
    highest = jnp.max(scores, axis=-1, keepdims=True)
    expd = jnp.exp(scores - highest)
    total = jnp.sum(expd, axis=-1, keepdims=True)
    return expd * (1.0 / total), highest + jnp.log(total)


def forward_kernel(slots, counts, used, *rest, classes, list_len, scale):
    queries_in, velocity_in = rest[:2]
    key_refs, value_refs = rest[2 : 2 + classes], rest[2 + classes : 2 + 2 * classes]
    (
        attn,
        lse,
        squares,
        queries,
        ref_velocity,
        key_pool,
        value_pool,
        sems,
        key_sems,
        value_sems,
    ) = rest[2 + 2 * classes :]
    bring((queries_in, velocity_in), (queries, ref_velocity), sems, 0, True)
    fetch(key_refs, key_pool, key_sems, used, True)
    fetch(value_refs, value_pool, value_sems, used, True)
    rows, cols = queries.shape
    eye = diagonal()
    bring((queries_in, velocity_in), (queries, ref_velocity), sems, 0, False)
    fetch(key_refs, key_pool, key_sems, used, False)
    for block in range(rows // BLK):
        span = slice(block * BLK, (block + 1) * BLK)
        total = jnp.zeros((BLK, 1), jnp.float32)
        for head in range(cols // HD):
            hs = slice(head * HD, (head + 1) * HD)
            keys = listed(key_pool, slots, block, list_len, hs)
            probs, log_sum = block_probs(queries[span, hs], keys, counts, block, list_len, scale)
            if block == 0 and head == 0:
                fetch(value_refs, value_pool, value_sems, used, False)
            values = listed(value_pool, slots, block, list_len, hs)
            out = matmul(probs.astype(jnp.bfloat16), values, NN)
            attn[span, hs] = out
            diff = out - ref_velocity[span, hs].astype(jnp.float32)
            total = total + jnp.sum(diff * diff, axis=1, keepdims=True)
            lse[block * 8 : block * 8 + 8, hs] = jnp.broadcast_to(as_row(log_sum, eye), (8, HD))
        squares[block : block + 1, :] = as_row(total, eye)


def upstream_kernel(squares, *rest):
    sources = rest[:4]
    grad, lse, attn, policy_grad, ref_velocity, sems = rest[4:]
    bring(sources, (lse, attn, policy_grad, ref_velocity), sems, 0, True)
    rows, cols = attn.shape
    eye = diagonal()
    weights = []
    for block in range(rows // BLK):
        kl = as_column(squares[block : block + 1, :], eye) / (HEADS * HD)
        weights.append(kl_weight / (1.0 + kl))
    bring(sources, (lse, attn, policy_grad, ref_velocity), sems, 0, False)
    row = lax.broadcasted_iota(jnp.int32, (8, HD), 0)
    tails = []
    for block in range(rows // BLK):
        span = slice(block * BLK, (block + 1) * BLK)
        parts = []
        for head in range(cols // HD):
            hs = slice(head * HD, (head + 1) * HD)
            out = attn[span, hs]
            diff = out - ref_velocity[span, hs].astype(jnp.float32)
            upstream = (policy_grad[span, hs].astype(jnp.float32) + diff * weights[block]).astype(
                jnp.bfloat16
            )
            grad[span, hs] = upstream
            delta = jnp.sum(upstream.astype(jnp.float32) * out, axis=1, keepdims=True)
            tail = jnp.zeros((8, HD), jnp.float32)
            stats = (
                lse[block * 8 : block * 8 + 8, hs],
                jnp.broadcast_to(as_row(delta, eye), (8, HD)),
            )
            for base, left in enumerate(stats):
                for piece in range(3):
                    rounded = left.astype(jnp.bfloat16).astype(jnp.float32)
                    tail = jnp.where(row == base * 3 + piece, rounded, tail)
                    left = left - rounded
            parts.append(tail)
        tails.append(jnp.concatenate(parts, axis=1))
    grad[rows : rows + TAIL, :] = jnp.concatenate(tails, axis=0).astype(jnp.bfloat16)


def query_kernel(slots, counts, used, *rest, classes, list_len, scale):
    sources = rest[:3]
    key_refs, value_refs = rest[3 : 3 + classes], rest[3 + classes : 3 + 2 * classes]
    (
        grad_queries,
        queries,
        grad,
        attn,
        key_pool,
        value_pool,
        sems,
        key_sems,
        value_sems,
    ) = rest[3 + 2 * classes :]
    bring(sources, (queries, grad, attn), sems, 0, True)
    fetch(key_refs, key_pool, key_sems, used, True)
    fetch(value_refs, value_pool, value_sems, used, True)
    rows, cols = queries.shape
    bring(sources, (queries, grad, attn), sems, 0, False)
    fetch(key_refs, key_pool, key_sems, used, False)
    for block in range(rows // BLK):
        span = slice(block * BLK, (block + 1) * BLK)
        for head in range(cols // HD):
            hs = slice(head * HD, (head + 1) * HD)
            keys = listed(key_pool, slots, block, list_len, hs)
            probs, _ = block_probs(queries[span, hs], keys, counts, block, list_len, scale)
            if block == 0 and head == 0:
                fetch(value_refs, value_pool, value_sems, used, False)
            values = listed(value_pool, slots, block, list_len, hs)
            upstream = grad[span, hs]
            delta = jnp.sum(upstream.astype(jnp.float32) * attn[span, hs], axis=1, keepdims=True)
            grad_probs = matmul(upstream, values, NT)
            grad_scores = (probs * (grad_probs - delta)).astype(jnp.bfloat16)
            grad_queries[span, hs] = (matmul(grad_scores, keys, NN) * scale).astype(jnp.bfloat16)


def naming_kernel(own, valid, *rest, classes, list_len, blocks, rows):
    query_refs = rest[:classes]
    names, lists, sems = rest[classes:]
    targets = [lists.at[pl.ds(position * TAIL, TAIL)] for position in range(classes)]
    sources = [ref.at[pl.ds(rows, TAIL), pl.ds(0, HD)] for ref in query_refs]
    bring(sources, targets, sems, 0, True)
    bring(sources, targets, sems, 0, False)
    names[...] = jnp.zeros_like(names)
    lane = lax.broadcasted_iota(jnp.int32, (TAIL, HD), 1)
    place = lax.broadcasted_iota(jnp.int32, (1, HD), 1)
    for position in range(classes):
        ids = lists[position * TAIL : (position + 1) * TAIL, :].astype(jnp.float32)
        row = jnp.zeros((1, HD), jnp.float32)
        for block in range(blocks):
            mine = (own[0] + block).astype(jnp.float32)
            hit = jnp.where((ids == mine) & (lane < list_len), 1.0, 0.0)
            hit = jnp.max(hit, axis=1, keepdims=True)
            for part in range(blocks):
                row = jnp.where(place == part * blocks + block, hit[part : part + 1], row)
        row = row * valid[position].astype(jnp.float32)
        names[position : position + 1, :] = row.astype(jnp.int32)


def key_kernel(names, counts, *rest, classes, scale):
    keys_in, values_in = rest[:2]
    query_refs, grad_refs = rest[2 : 2 + classes], rest[2 + classes : 2 + 2 * classes]
    (
        grad_keys,
        grad_values,
        keys,
        values,
        query_pool,
        grad_pool,
        acc_k,
        acc_v,
        entries,
        used,
        sems,
        query_sems,
        grad_sems,
    ) = rest[2 + 2 * classes :]
    rows, cols = keys.shape
    blocks = rows // BLK
    height = rows + TAIL
    bring((keys_in, values_in), (keys, values), sems, 0, True)
    for position in range(classes):
        total = names[position, 0]
        for place in range(1, blocks * blocks):
            total = total + names[position, place]
        used[position] = total
    fetch(query_refs, query_pool, query_sems, used, True)
    fetch(grad_refs, grad_pool, grad_sems, used, True)
    lengths = []
    for block in range(blocks):

        def collect(entry, length, block=block):
            hit = names[entry // blocks, (entry % blocks) * blocks + block]
            entries[block, length] = entry
            return length + hit

        length = lax.fori_loop(0, classes * blocks, collect, jnp.int32(0))
        entries[block, length] = 0
        lengths.append(length)
    acc_k[...] = jnp.zeros_like(acc_k)
    acc_v[...] = jnp.zeros_like(acc_v)
    bring((keys_in, values_in), (keys, values), sems, 0, False)
    fetch(query_refs, query_pool, query_sems, used, False)
    fetch(grad_refs, grad_pool, grad_sems, used, False)
    row_in_block = lax.broadcasted_iota(jnp.int32, (BLK, WIDE * BLK), 0)
    for block in range(blocks):
        key_rows = slice(block * BLK, (block + 1) * BLK)
        valid = row_in_block < counts[block]
        length = lengths[block]

        def step(chunk, carry, block=block, key_rows=key_rows, valid=valid, length=length):
            places = []
            for lane in range(WIDE):
                index = chunk * WIDE + lane
                live = index < length
                entry = jnp.where(live, entries[block, jnp.minimum(index, length)], 0)
                position, part = entry // blocks, entry % blocks
                places.append(
                    (
                        pl.ds(pl.multiple_of(position * height + part * BLK, 16), BLK),
                        pl.ds(pl.multiple_of(position * height + rows, 16), TAIL),
                        part == 0,
                        jnp.where(live, 0.0, 1e30),
                    )
                )
            for head in range(cols // HD):
                hs = slice(head * HD, (head + 1) * HD)
                query = jnp.concatenate([query_pool[p[0], hs] for p in places], axis=0)
                upstream = jnp.concatenate([grad_pool[p[0], hs] for p in places], axis=0)
                sums, deltas = [], []
                for _, stat_rows, first, extra in places:
                    stats = grad_pool[stat_rows, hs].astype(jnp.float32)
                    stats = jnp.where(first, stats[:8], stats[8:])
                    sums.append(stats[0:1] + stats[1:2] + stats[2:3] + extra)
                    deltas.append(stats[3:4] + stats[4:5] + stats[5:6])
                log_sum = jnp.concatenate(sums, axis=1)
                delta = jnp.concatenate(deltas, axis=1)
                scores = matmul(keys[key_rows, hs], query, NT) * scale - log_sum
                probs = jnp.exp(jnp.where(valid, scores, -1e30))
                grad_probs = matmul(values[key_rows, hs], upstream, NT)
                grad_scores = (probs * (grad_probs - delta)).astype(jnp.bfloat16)
                acc_v[key_rows, hs] += matmul(probs.astype(jnp.bfloat16), upstream, NN)
                acc_k[key_rows, hs] += matmul(grad_scores, query, NN)
            return carry

        lax.fori_loop(0, (length + WIDE - 1) // WIDE, step, 0)
        grad_keys[key_rows, :] = (acc_k[key_rows, :] * scale).astype(jnp.bfloat16)
        grad_values[key_rows, :] = acc_v[key_rows, :].astype(jnp.bfloat16)


SMEM = pl.BlockSpec(memory_space=pltpu.SMEM)
VMEM = pl.BlockSpec(memory_space=pltpu.VMEM)
ANY = pl.BlockSpec(memory_space=pl.ANY)


FRAMES = 32
GRID = [(z, y, x) for z in range(2) for y in range(4) for x in range(4)]


def at(z, y, x):
    return z * 16 + y * 4 + x


def flip(bit):
    return [(f, f ^ bit) for f in range(FRAMES)]


def carry_pairs(bit, keep):
    pairs = []
    for f in range(FRAMES):
        if f & bit and f + bit < FRAMES and keep(f, f + bit):
            pairs += [(f, f + bit), (f + bit, f)]
    return pairs


def any_pair(f, g):
    return True


def same_half(f, g):
    return f >> 4 == g >> 4


DIRECT = [
    ("half", "own", flip(16)),
    ("step8", "own", carry_pairs(8, any_pair)),
    ("flip8", "own", flip(8)),
    ("flip4", "own", flip(4)),
    ("step4", "own", carry_pairs(4, same_half)),
    ("flip2", "own", flip(2)),
    ("flip1", "own", flip(1)),
    ("step1", "own", carry_pairs(1, same_half)),
]
RELAYED = [
    (
        "wrap4",
        "half",
        [(at(1, 3, x), at(1, 0, x)) for x in range(4)]
        + [(at(0, 0, x), at(0, 3, x)) for x in range(4)],
    ),
    (
        "wrap2",
        "step8",
        [
            (at(1, 1, 2), at(1, 0, 0)),
            (at(1, 1, 3), at(1, 0, 1)),
            (at(0, 2, 0), at(0, 3, 2)),
            (at(0, 2, 1), at(0, 3, 3)),
        ],
    ),
    ("wrap1", "step8", [(at(1, 1, 3), at(1, 0, 0)), (at(0, 2, 0), at(0, 3, 3))]),
    (
        "row2",
        "turn",
        [(at(z, y, x), at(z, y, x - 2)) for z, y, x in GRID if y > 0 and x > 1]
        + [(at(z, y, x), at(z, y, x + 2)) for z, y, x in GRID if y < 3 and x < 2],
    ),
]
NAMES = ["own"] + [name for name, _, _ in DIRECT + RELAYED]


def turn_takes_flip(f):
    return (f & 3 >= 2) == (f >> 2 & 1 == 1)


def owners():
    held = {"own": list(range(FRAMES))}
    for name, sent, pairs in DIRECT + RELAYED:
        if sent == "turn":
            held["turn"] = [
                held["flip4" if turn_takes_flip(f) else "step4"][f] for f in range(FRAMES)
            ]
        held[name] = [-1] * FRAMES
        for source, target in pairs:
            held[name][target] = held[sent][source]
    table = np.array([held[name] for name in NAMES])
    for f in range(FRAMES):
        got = sorted(o for o in table[:, f] if o >= 0)
        near = {f + s * (1 << level) for level in range(5) for s in (1, -1)} | {f}
        assert got == sorted(o for o in near if 0 <= o < FRAMES)
    return table


def spread(value, turn_flip):
    held = {"own": value}
    for name, sent, pairs in DIRECT + RELAYED:
        if sent == "turn" and "turn" not in held:
            held["turn"] = jnp.where(turn_flip, held["flip4"], held["step4"])
        held[name] = lax.ppermute(held[sent], "frame", pairs)
    return [held[name] for name in NAMES]


def local(queries, keys, values, policy_grad, ref_velocity, key_lists, frame_tokens):
    rows, cols = queries.shape
    blocks = rows // BLK
    list_len = key_lists.shape[1]
    all_blocks = frame_tokens.shape[0]
    scale = 1.0 / math.sqrt(HD)
    assert lax.axis_size("frame") == FRAMES
    me = lax.axis_index("frame")
    classes = len(NAMES)
    f32 = jnp.float32
    turn_flip = (me % 4 >= 2) == (me // 4 % 2 == 1)

    key_pool = spread(keys, turn_flip)
    value_pool = spread(values, turn_flip)
    lists16 = jnp.pad(
        key_lists.astype(jnp.bfloat16), ((0, TAIL - blocks), (0, cols - list_len))
    )
    tailed = jnp.concatenate([queries, lists16], axis=0)
    tailed, last = lax.optimization_barrier((tailed, key_pool + value_pool))
    key_pool, value_pool = last[:classes], last[classes:]
    query_pool = spread(tailed, turn_flip)

    owner_here = lax.dynamic_slice(
        jnp.asarray(owners().T.astype(np.int32)), (me, 0), (1, classes)
    ).reshape(-1)
    owner = key_lists // blocks
    hits = owner[..., None] == owner_here
    slots = jnp.sum(jnp.where(hits, jnp.arange(classes, dtype=jnp.int32), 0), axis=-1)
    slots = (slots * blocks + key_lists % blocks).reshape(-1)
    used = jnp.any(hits, axis=(0, 1)).astype(jnp.int32)
    valid = (owner_here >= 0).astype(jnp.int32)
    ids = jnp.arange(all_blocks, dtype=jnp.int32)
    counts = jnp.sum(jnp.where(key_lists[..., None] == ids, frame_tokens, 0), axis=-1).reshape(-1)
    own = me * blocks + jnp.arange(blocks, dtype=jnp.int32)
    own_counts = jnp.sum(jnp.where(own[:, None] == ids, frame_tokens, 0), axis=-1)

    def shard(dtype=jnp.bfloat16, height=rows):
        return pltpu.VMEM((height, cols), dtype)

    def dma(count):
        return pltpu.SemaphoreType.DMA((count,))

    pools = [shard(height=classes * rows)] * 2
    params = pltpu.CompilerParams(vmem_limit_bytes=48 << 20)
    attn, lse, squares = pl.pallas_call(
        functools.partial(forward_kernel, classes=classes, list_len=list_len, scale=scale),
        out_shape=(
            jax.ShapeDtypeStruct((rows, cols), f32),
            jax.ShapeDtypeStruct((blocks * 8, cols), f32),
            jax.ShapeDtypeStruct((blocks, BLK), f32),
        ),
        in_specs=[SMEM] * 3 + [ANY] * (2 + 2 * classes),
        out_specs=(VMEM, VMEM, VMEM),
        scratch_shapes=[shard(), shard()] + pools + [dma(2), dma(classes), dma(classes)],
        compiler_params=params,
        name="forward",
    )(slots, counts, used, queries, ref_velocity, *key_pool, *value_pool)

    heads = lax.axis_size("head")
    step = 1
    while step < heads:
        squares = squares + lax.ppermute(squares, "head", [(i, i ^ step) for i in range(heads)])
        step *= 2

    grad = pl.pallas_call(
        upstream_kernel,
        out_shape=jax.ShapeDtypeStruct((rows + TAIL, cols), jnp.bfloat16),
        in_specs=[VMEM] + [ANY] * 4,
        out_specs=VMEM,
        scratch_shapes=[shard(f32, blocks * 8), shard(f32), shard(), shard(), dma(4)],
        compiler_params=params,
        name="upstream",
    )(squares, lse, attn, policy_grad, ref_velocity)

    grad_pool = spread(grad, turn_flip)

    names = pl.pallas_call(
        functools.partial(
            naming_kernel, classes=classes, list_len=list_len, blocks=blocks, rows=rows
        ),
        out_shape=jax.ShapeDtypeStruct((16, HD), jnp.int32),
        in_specs=[SMEM, SMEM] + [ANY] * classes,
        out_specs=VMEM,
        scratch_shapes=[pltpu.VMEM((classes * TAIL, HD), jnp.bfloat16), dma(classes)],
        compiler_params=params,
        name="naming",
    )(own, valid, *query_pool)

    grad_queries = pl.pallas_call(
        functools.partial(query_kernel, classes=classes, list_len=list_len, scale=scale),
        out_shape=jax.ShapeDtypeStruct((rows, cols), jnp.bfloat16),
        in_specs=[SMEM] * 3 + [ANY] * (3 + 2 * classes),
        out_specs=VMEM,
        scratch_shapes=[shard(), shard(height=rows + TAIL), shard(f32)]
        + pools
        + [dma(3), dma(classes), dma(classes)],
        compiler_params=params,
        name="grad_queries",
    )(slots, counts, used, queries, grad, attn, *key_pool, *value_pool)

    grad_keys, grad_values = pl.pallas_call(
        functools.partial(key_kernel, classes=classes, scale=scale),
        out_shape=(
            jax.ShapeDtypeStruct((rows, cols), jnp.bfloat16),
            jax.ShapeDtypeStruct((rows, cols), jnp.bfloat16),
        ),
        in_specs=[SMEM, SMEM] + [ANY] * (2 + 2 * classes),
        out_specs=(VMEM, VMEM),
        scratch_shapes=[shard(), shard()]
        + [shard(height=classes * (rows + TAIL))] * 2
        + [
            shard(f32),
            shard(f32),
            pltpu.SMEM((blocks, 32), jnp.int32),
            pltpu.SMEM((classes,), jnp.int32),
            dma(2),
            dma(classes),
            dma(classes),
        ],
        compiler_params=params,
        name="grad_keys_values",
    )(names, own_counts, keys, values, *query_pool, *grad_pool)
    return grad_queries, grad_keys, grad_values


def solution(mesh):
    in_specs = (
        P("frame", "head"),
        P("frame", "head"),
        P("frame", "head"),
        P("frame", "head"),
        P("frame", "head"),
        P("frame", None),
        P(),
    )
    out_specs = (P("frame", "head"), P("frame", "head"), P("frame", "head"))
    return jax.shard_map(local, mesh=mesh, in_specs=in_specs, out_specs=out_specs, check_vma=False)
```

```python
import functools
import math

import jax
import jax.numpy as jnp
import numpy as np
from jax import lax
from jax.experimental import pallas as pl
from jax.experimental.pallas import tpu as pltpu
from jax.sharding import PartitionSpec as P

HEADS = 40
HD = 128
BLK = 128
TAIL = 16

kl_weight = 1.0


WIDE = 2

NT = (((1,), (1,)), ((), ()))
NN = (((1,), (0,)), ((), ()))


def matmul(left, right, dims):
    return lax.dot_general(left, right, dims, preferred_element_type=jnp.float32)


def diagonal():
    return lax.broadcasted_iota(jnp.int32, (BLK, BLK), 0) == lax.broadcasted_iota(
        jnp.int32, (BLK, BLK), 1
    )


def as_row(column, eye):
    return jnp.sum(jnp.where(eye, column, 0.0), axis=0, keepdims=True)


def as_column(row, eye):
    return jnp.sum(jnp.where(eye, row, 0.0), axis=1, keepdims=True)


def bring(sources, targets, sems, first, start):
    for position, (source, target) in enumerate(zip(sources, targets)):
        copy = pltpu.make_async_copy(source, target, sems.at[first + position])
        if start:
            copy.start()
        else:
            copy.wait()


def fetch(sources, pool, sems, used, start):
    height = pool.shape[0] // len(sources)
    for position, source in enumerate(sources):

        @pl.when(used[position] != 0)
        def _():
            copy = pltpu.make_async_copy(
                source, pool.at[pl.ds(position * height, height)], sems.at[position]
            )
            if start:
                copy.start()
            else:
                copy.wait()


def listed(pool, slots, block, list_len, cols):
    return jnp.concatenate(
        [
            pool[pl.ds(pl.multiple_of(slots[block * list_len + s] * BLK, BLK), BLK), cols]
            for s in range(list_len)
        ],
        axis=0,
    )


def block_probs(query, key_block, counts, block, list_len, scale):
    scores = matmul(query, key_block, NT) * scale
    lane = lax.broadcasted_iota(jnp.int32, (BLK, BLK), 1)
    scores = jnp.concatenate(
        [
            jnp.where(
                lane < counts[block * list_len + s], scores[:, s * BLK : (s + 1) * BLK], -1e30
            )
            for s in range(list_len)
        ],
        axis=1,
    )
    highest = jnp.max(scores, axis=-1, keepdims=True)
    expd = jnp.exp(scores - highest)
    total = jnp.sum(expd, axis=-1, keepdims=True)
    return expd * (1.0 / total), highest + jnp.log(total)


def forward_kernel(slots, counts, used, *rest, classes, list_len, scale):
    queries_in, velocity_in = rest[:2]
    key_refs, value_refs = rest[2 : 2 + classes], rest[2 + classes : 2 + 2 * classes]
    (
        attn,
        lse,
        squares,
        queries,
        ref_velocity,
        key_pool,
        value_pool,
        sems,
        key_sems,
        value_sems,
    ) = rest[2 + 2 * classes :]
    bring((queries_in, velocity_in), (queries, ref_velocity), sems, 0, True)
    fetch(key_refs, key_pool, key_sems, used, True)
    fetch(value_refs, value_pool, value_sems, used, True)
    rows, cols = queries.shape
    eye = diagonal()
    bring((queries_in, velocity_in), (queries, ref_velocity), sems, 0, False)
    fetch(key_refs, key_pool, key_sems, used, False)
    for block in range(rows // BLK):
        span = slice(block * BLK, (block + 1) * BLK)
        total = jnp.zeros((BLK, 1), jnp.float32)
        for head in range(cols // HD):
            hs = slice(head * HD, (head + 1) * HD)
            keys = listed(key_pool, slots, block, list_len, hs)
            probs, log_sum = block_probs(queries[span, hs], keys, counts, block, list_len, scale)
            if block == 0 and head == 0:
                fetch(value_refs, value_pool, value_sems, used, False)
            values = listed(value_pool, slots, block, list_len, hs)
            out = matmul(probs.astype(jnp.bfloat16), values, NN)
            attn[span, hs] = out
            diff = out - ref_velocity[span, hs].astype(jnp.float32)
            total = total + jnp.sum(diff * diff, axis=1, keepdims=True)
            lse[block * 8 : block * 8 + 8, hs] = jnp.broadcast_to(as_row(log_sum, eye), (8, HD))
        squares[block : block + 1, :] = as_row(total, eye)


def upstream_kernel(squares, *rest):
    sources = rest[:4]
    grad, lse, attn, policy_grad, ref_velocity, sems = rest[4:]
    bring(sources, (lse, attn, policy_grad, ref_velocity), sems, 0, True)
    rows, cols = attn.shape
    eye = diagonal()
    weights = []
    for block in range(rows // BLK):
        kl = as_column(squares[block : block + 1, :], eye) / (HEADS * HD)
        weights.append(kl_weight / (1.0 + kl))
    bring(sources, (lse, attn, policy_grad, ref_velocity), sems, 0, False)
    row = lax.broadcasted_iota(jnp.int32, (8, HD), 0)
    tails = []
    for block in range(rows // BLK):
        span = slice(block * BLK, (block + 1) * BLK)
        parts = []
        for head in range(cols // HD):
            hs = slice(head * HD, (head + 1) * HD)
            out = attn[span, hs]
            diff = out - ref_velocity[span, hs].astype(jnp.float32)
            upstream = (policy_grad[span, hs].astype(jnp.float32) + diff * weights[block]).astype(
                jnp.bfloat16
            )
            grad[span, hs] = upstream
            delta = jnp.sum(upstream.astype(jnp.float32) * out, axis=1, keepdims=True)
            tail = jnp.zeros((8, HD), jnp.float32)
            stats = (
                lse[block * 8 : block * 8 + 8, hs],
                jnp.broadcast_to(as_row(delta, eye), (8, HD)),
            )
            for base, left in enumerate(stats):
                for piece in range(3):
                    rounded = left.astype(jnp.bfloat16).astype(jnp.float32)
                    tail = jnp.where(row == base * 3 + piece, rounded, tail)
                    left = left - rounded
            parts.append(tail)
        tails.append(jnp.concatenate(parts, axis=1))
    grad[rows : rows + TAIL, :] = jnp.concatenate(tails, axis=0).astype(jnp.bfloat16)


def query_kernel(slots, counts, used, *rest, classes, list_len, scale):
    sources = rest[:3]
    key_refs, value_refs = rest[3 : 3 + classes], rest[3 + classes : 3 + 2 * classes]
    (
        grad_queries,
        queries,
        grad,
        attn,
        key_pool,
        value_pool,
        sems,
        key_sems,
        value_sems,
    ) = rest[3 + 2 * classes :]
    bring(sources, (queries, grad, attn), sems, 0, True)
    fetch(key_refs, key_pool, key_sems, used, True)
    fetch(value_refs, value_pool, value_sems, used, True)
    rows, cols = queries.shape
    bring(sources, (queries, grad, attn), sems, 0, False)
    fetch(key_refs, key_pool, key_sems, used, False)
    for block in range(rows // BLK):
        span = slice(block * BLK, (block + 1) * BLK)
        for head in range(cols // HD):
            hs = slice(head * HD, (head + 1) * HD)
            keys = listed(key_pool, slots, block, list_len, hs)
            probs, _ = block_probs(queries[span, hs], keys, counts, block, list_len, scale)
            if block == 0 and head == 0:
                fetch(value_refs, value_pool, value_sems, used, False)
            values = listed(value_pool, slots, block, list_len, hs)
            upstream = grad[span, hs]
            delta = jnp.sum(upstream.astype(jnp.float32) * attn[span, hs], axis=1, keepdims=True)
            grad_probs = matmul(upstream, values, NT)
            grad_scores = (probs * (grad_probs - delta)).astype(jnp.bfloat16)
            grad_queries[span, hs] = (matmul(grad_scores, keys, NN) * scale).astype(jnp.bfloat16)


def naming_kernel(own, valid, *rest, classes, list_len, blocks, rows):
    query_refs = rest[:classes]
    names, lists, sems = rest[classes:]
    targets = [lists.at[pl.ds(position * TAIL, TAIL)] for position in range(classes)]
    sources = [ref.at[pl.ds(rows, TAIL), pl.ds(0, HD)] for ref in query_refs]
    bring(sources, targets, sems, 0, True)
    bring(sources, targets, sems, 0, False)
    names[...] = jnp.zeros_like(names)
    lane = lax.broadcasted_iota(jnp.int32, (TAIL, HD), 1)
    place = lax.broadcasted_iota(jnp.int32, (1, HD), 1)
    for position in range(classes):
        ids = lists[position * TAIL : (position + 1) * TAIL, :].astype(jnp.float32)
        row = jnp.zeros((1, HD), jnp.float32)
        for block in range(blocks):
            mine = (own[0] + block).astype(jnp.float32)
            hit = jnp.where((ids == mine) & (lane < list_len), 1.0, 0.0)
            hit = jnp.max(hit, axis=1, keepdims=True)
            for part in range(blocks):
                row = jnp.where(place == part * blocks + block, hit[part : part + 1], row)
        row = row * valid[position].astype(jnp.float32)
        names[position : position + 1, :] = row.astype(jnp.int32)


def key_kernel(names, counts, *rest, classes, scale):
    keys_in, values_in = rest[:2]
    query_refs, grad_refs = rest[2 : 2 + classes], rest[2 + classes : 2 + 2 * classes]
    (
        grad_keys,
        grad_values,
        keys,
        values,
        query_pool,
        grad_pool,
        acc_k,
        acc_v,
        entries,
        used,
        sems,
        query_sems,
        grad_sems,
    ) = rest[2 + 2 * classes :]
    rows, cols = keys.shape
    blocks = rows // BLK
    height = rows + TAIL
    bring((keys_in, values_in), (keys, values), sems, 0, True)
    for position in range(classes):
        total = names[position, 0]
        for place in range(1, blocks * blocks):
            total = total + names[position, place]
        used[position] = total
    fetch(query_refs, query_pool, query_sems, used, True)
    fetch(grad_refs, grad_pool, grad_sems, used, True)
    lengths = []
    for block in range(blocks):

        def collect(entry, length, block=block):
            hit = names[entry // blocks, (entry % blocks) * blocks + block]
            entries[block, length] = entry
            return length + hit

        length = lax.fori_loop(0, classes * blocks, collect, jnp.int32(0))
        entries[block, length] = 0
        lengths.append(length)
    acc_k[...] = jnp.zeros_like(acc_k)
    acc_v[...] = jnp.zeros_like(acc_v)
    bring((keys_in, values_in), (keys, values), sems, 0, False)
    fetch(query_refs, query_pool, query_sems, used, False)
    fetch(grad_refs, grad_pool, grad_sems, used, False)
    row_in_block = lax.broadcasted_iota(jnp.int32, (BLK, WIDE * BLK), 0)
    for block in range(blocks):
        key_rows = slice(block * BLK, (block + 1) * BLK)
        valid = row_in_block < counts[block]
        length = lengths[block]

        def step(chunk, carry, block=block, key_rows=key_rows, valid=valid, length=length):
            places = []
            for lane in range(WIDE):
                index = chunk * WIDE + lane
                live = index < length
                entry = jnp.where(live, entries[block, jnp.minimum(index, length)], 0)
                position, part = entry // blocks, entry % blocks
                places.append(
                    (
                        pl.ds(pl.multiple_of(position * height + part * BLK, 16), BLK),
                        pl.ds(pl.multiple_of(position * height + rows, 16), TAIL),
                        part == 0,
                        jnp.where(live, 0.0, 1e30),
                    )
                )
            for head in range(cols // HD):
                hs = slice(head * HD, (head + 1) * HD)
                query = jnp.concatenate([query_pool[p[0], hs] for p in places], axis=0)
                upstream = jnp.concatenate([grad_pool[p[0], hs] for p in places], axis=0)
                sums, deltas = [], []
                for _, stat_rows, first, extra in places:
                    stats = grad_pool[stat_rows, hs].astype(jnp.float32)
                    stats = jnp.where(first, stats[:8], stats[8:])
                    sums.append(stats[0:1] + stats[1:2] + stats[2:3] + extra)
                    deltas.append(stats[3:4] + stats[4:5] + stats[5:6])
                log_sum = jnp.concatenate(sums, axis=1)
                delta = jnp.concatenate(deltas, axis=1)
                scores = matmul(keys[key_rows, hs], query, NT) * scale - log_sum
                probs = jnp.exp(jnp.where(valid, scores, -1e30))
                grad_probs = matmul(values[key_rows, hs], upstream, NT)
                grad_scores = (probs * (grad_probs - delta)).astype(jnp.bfloat16)
                acc_v[key_rows, hs] += matmul(probs.astype(jnp.bfloat16), upstream, NN)
                acc_k[key_rows, hs] += matmul(grad_scores, query, NN)
            return carry

        lax.fori_loop(0, (length + WIDE - 1) // WIDE, step, 0)
        grad_keys[key_rows, :] = (acc_k[key_rows, :] * scale).astype(jnp.bfloat16)
        grad_values[key_rows, :] = acc_v[key_rows, :].astype(jnp.bfloat16)


SMEM = pl.BlockSpec(memory_space=pltpu.SMEM)
VMEM = pl.BlockSpec(memory_space=pltpu.VMEM)
ANY = pl.BlockSpec(memory_space=pltpu.HBM)


FRAMES = 32
GRID = [(z, y, x) for z in range(2) for y in range(4) for x in range(4)]


def at(z, y, x):
    return z * 16 + y * 4 + x


def flip(bit):
    return [(f, f ^ bit) for f in range(FRAMES)]


def carry_pairs(bit, keep):
    pairs = []
    for f in range(FRAMES):
        if f & bit and f + bit < FRAMES and keep(f, f + bit):
            pairs += [(f, f + bit), (f + bit, f)]
    return pairs


def any_pair(f, g):
    return True


def same_half(f, g):
    return f >> 4 == g >> 4


DIRECT = [
    ("half", "own", flip(16)),
    ("step8", "own", carry_pairs(8, any_pair)),
    ("flip8", "own", flip(8)),
    ("flip4", "own", flip(4)),
    ("step4", "own", carry_pairs(4, same_half)),
    ("flip2", "own", flip(2)),
    ("flip1", "own", flip(1)),
    ("step1", "own", carry_pairs(1, same_half)),
]
RELAYED = [
    (
        "wrap4",
        "half",
        [(at(1, 3, x), at(1, 0, x)) for x in range(4)]
        + [(at(0, 0, x), at(0, 3, x)) for x in range(4)],
    ),
    (
        "wrap2",
        "step8",
        [
            (at(1, 1, 2), at(1, 0, 0)),
            (at(1, 1, 3), at(1, 0, 1)),
            (at(0, 2, 0), at(0, 3, 2)),
            (at(0, 2, 1), at(0, 3, 3)),
        ],
    ),
    ("wrap1", "step8", [(at(1, 1, 3), at(1, 0, 0)), (at(0, 2, 0), at(0, 3, 3))]),
    (
        "row2",
        "turn",
        [(at(z, y, x), at(z, y, x - 2)) for z, y, x in GRID if y > 0 and x > 1]
        + [(at(z, y, x), at(z, y, x + 2)) for z, y, x in GRID if y < 3 and x < 2],
    ),
]
NAMES = ["own"] + [name for name, _, _ in DIRECT + RELAYED]


def turn_takes_flip(f):
    return (f & 3 >= 2) == (f >> 2 & 1 == 1)


def owners():
    held = {"own": list(range(FRAMES))}
    for name, sent, pairs in DIRECT + RELAYED:
        if sent == "turn":
            held["turn"] = [
                held["flip4" if turn_takes_flip(f) else "step4"][f] for f in range(FRAMES)
            ]
        held[name] = [-1] * FRAMES
        for source, target in pairs:
            held[name][target] = held[sent][source]
    table = np.array([held[name] for name in NAMES])
    for f in range(FRAMES):
        got = sorted(o for o in table[:, f] if o >= 0)
        near = {f + s * (1 << level) for level in range(5) for s in (1, -1)} | {f}
        assert got == sorted(o for o in near if 0 <= o < FRAMES)
    return table


def spread(value, turn_flip):
    held = {"own": value}
    for name, sent, pairs in DIRECT + RELAYED:
        if sent == "turn" and "turn" not in held:
            held["turn"] = jnp.where(turn_flip, held["flip4"], held["step4"])
        held[name] = lax.ppermute(held[sent], "frame", pairs)
    return [held[name] for name in NAMES]


def step(queries, keys, values, policy_grad, ref_velocity, key_lists, frame_tokens):
    rows, cols = queries.shape
    blocks = rows // BLK
    list_len = key_lists.shape[1]
    all_blocks = frame_tokens.shape[0]
    scale = 1.0 / math.sqrt(HD)
    assert lax.axis_size("frame") == FRAMES
    me = lax.axis_index("frame")
    classes = len(NAMES)
    f32 = jnp.float32
    turn_flip = (me % 4 >= 2) == (me // 4 % 2 == 1)

    key_pool = spread(keys, turn_flip)
    value_pool = spread(values, turn_flip)

    owner_here = lax.dynamic_slice(
        jnp.asarray(owners().T.astype(np.int32)), (me, 0), (1, classes)
    ).reshape(-1)
    owner = key_lists // blocks
    hits = owner[..., None] == owner_here
    slots = jnp.sum(jnp.where(hits, jnp.arange(classes, dtype=jnp.int32), 0), axis=-1)
    slots = (slots * blocks + key_lists % blocks).reshape(-1)
    used = jnp.any(hits, axis=(0, 1)).astype(jnp.int32)
    valid = (owner_here >= 0).astype(jnp.int32)
    ids = jnp.arange(all_blocks, dtype=jnp.int32)
    counts = jnp.sum(jnp.where(key_lists[..., None] == ids, frame_tokens, 0), axis=-1).reshape(-1)
    own = me * blocks + jnp.arange(blocks, dtype=jnp.int32)
    own_counts = jnp.sum(jnp.where(own[:, None] == ids, frame_tokens, 0), axis=-1)

    lists16 = jnp.pad(
        key_lists.astype(jnp.bfloat16), ((0, TAIL - blocks), (0, cols - list_len))
    )
    tailed = jnp.concatenate([queries, lists16], axis=0)
    tailed, slots, counts, used, valid, own, own_counts = lax.optimization_barrier(
        (tailed, slots, counts, used, valid, own, own_counts)
    )
    query_pool = spread(tailed, turn_flip)

    def shard(dtype=jnp.bfloat16, height=rows):
        return pltpu.VMEM((height, cols), dtype)

    def dma(count):
        return pltpu.SemaphoreType.DMA((count,))

    pools = [shard(height=classes * rows)] * 2
    params = pltpu.CompilerParams(vmem_limit_bytes=48 << 20)
    attn, lse, squares = pl.pallas_call(
        functools.partial(forward_kernel, classes=classes, list_len=list_len, scale=scale),
        out_shape=(
            jax.ShapeDtypeStruct((rows, cols), f32),
            jax.ShapeDtypeStruct((blocks * 8, cols), f32),
            jax.ShapeDtypeStruct((blocks, BLK), f32),
        ),
        in_specs=[SMEM] * 3 + [ANY] * (2 + 2 * classes),
        out_specs=(VMEM, VMEM, VMEM),
        scratch_shapes=[shard(), shard()] + pools + [dma(2), dma(classes), dma(classes)],
        compiler_params=params,
        name="forward",
    )(slots, counts, used, queries, ref_velocity, *key_pool, *value_pool)

    heads = lax.axis_size("head")
    hop = 1
    while hop < heads:
        squares = squares + lax.ppermute(squares, "head", [(i, i ^ hop) for i in range(heads)])
        hop *= 2

    grad = pl.pallas_call(
        upstream_kernel,
        out_shape=jax.ShapeDtypeStruct((rows + TAIL, cols), jnp.bfloat16),
        in_specs=[VMEM] + [ANY] * 4,
        out_specs=VMEM,
        scratch_shapes=[shard(f32, blocks * 8), shard(f32), shard(), shard(), dma(4)],
        compiler_params=params,
        name="upstream",
    )(squares, lse, attn, policy_grad, ref_velocity)

    grad_pool = spread(grad, turn_flip)

    names = pl.pallas_call(
        functools.partial(
            naming_kernel, classes=classes, list_len=list_len, blocks=blocks, rows=rows
        ),
        out_shape=jax.ShapeDtypeStruct((16, HD), jnp.int32),
        in_specs=[SMEM, SMEM] + [ANY] * classes,
        out_specs=VMEM,
        scratch_shapes=[pltpu.VMEM((classes * TAIL, HD), jnp.bfloat16), dma(classes)],
        compiler_params=params,
        name="naming",
    )(own, valid, *query_pool)

    grad_queries = pl.pallas_call(
        functools.partial(query_kernel, classes=classes, list_len=list_len, scale=scale),
        out_shape=jax.ShapeDtypeStruct((rows, cols), jnp.bfloat16),
        in_specs=[SMEM] * 3 + [ANY] * (3 + 2 * classes),
        out_specs=VMEM,
        scratch_shapes=[shard(), shard(height=rows + TAIL), shard(f32)]
        + pools
        + [dma(3), dma(classes), dma(classes)],
        compiler_params=params,
        name="grad_queries",
    )(slots, counts, used, queries, grad, attn, *key_pool, *value_pool)

    grad_keys, grad_values = pl.pallas_call(
        functools.partial(key_kernel, classes=classes, scale=scale),
        out_shape=(
            jax.ShapeDtypeStruct((rows, cols), jnp.bfloat16),
            jax.ShapeDtypeStruct((rows, cols), jnp.bfloat16),
        ),
        in_specs=[SMEM, SMEM] + [ANY] * (2 + 2 * classes),
        out_specs=(VMEM, VMEM),
        scratch_shapes=[shard(), shard()]
        + [shard(height=classes * (rows + TAIL))] * 2
        + [
            shard(f32),
            shard(f32),
            pltpu.SMEM((blocks, 32), jnp.int32),
            pltpu.SMEM((classes,), jnp.int32),
            dma(2),
            dma(classes),
            dma(classes),
        ],
        compiler_params=params,
        name="grad_keys_values",
    )(names, own_counts, keys, values, *query_pool, *grad_pool)
    return grad_queries, grad_keys, grad_values


def solution(mesh):
    in_specs = (
        P("frame", "head"),
        P("frame", "head"),
        P("frame", "head"),
        P("frame", "head"),
        P("frame", "head"),
        P("frame", None),
        P(),
    )
    out_specs = (P("frame", "head"), P("frame", "head"), P("frame", "head"))
    return jax.shard_map(step, mesh=mesh, in_specs=in_specs, out_specs=out_specs, check_vma=False)
```

```python
import functools
import math

import jax
import jax.numpy as jnp
import numpy as np
from jax import lax
from jax.experimental import pallas as pl
from jax.experimental.pallas import tpu as pltpu
from jax.sharding import PartitionSpec as P

HEADS = 40
HD = 128
BLK = 128
TAIL = 16

kl_weight = 1.0
LOG2E = 1.4426950408889634


WIDE = 4

NT = (((1,), (1,)), ((), ()))
NN = (((1,), (0,)), ((), ()))


def matmul(left, right, dims):
    return lax.dot_general(left, right, dims, preferred_element_type=jnp.float32)


def diagonal():
    return lax.broadcasted_iota(jnp.int32, (BLK, BLK), 0) == lax.broadcasted_iota(
        jnp.int32, (BLK, BLK), 1
    )


def as_row(column, eye):
    return jnp.sum(jnp.where(eye, column, 0.0), axis=0, keepdims=True)


def as_column(row, eye):
    return jnp.sum(jnp.where(eye, row, 0.0), axis=1, keepdims=True)


def bring(sources, targets, sems, first, start):
    for position, (source, target) in enumerate(zip(sources, targets)):
        copy = pltpu.make_async_copy(source, target, sems.at[first + position])
        if start:
            copy.start()
        else:
            copy.wait()


def fetch(sources, pool, sems, used, start):
    height = pool.shape[0] // len(sources)
    for position, source in enumerate(sources):

        @pl.when(used[position] != 0)
        def _():
            copy = pltpu.make_async_copy(
                source, pool.at[pl.ds(position * height, height)], sems.at[position]
            )
            if start:
                copy.start()
            else:
                copy.wait()


def listed(pool, slots, block, list_len, cols):
    return jnp.concatenate(
        [
            pool[pl.ds(pl.multiple_of(slots[block * list_len + s] * BLK, BLK), BLK), cols]
            for s in range(list_len)
        ],
        axis=0,
    )


def block_exps(query, key_block, counts, block, list_len, scale):
    scores = matmul(query, key_block, NT)
    lane = lax.broadcasted_iota(jnp.int32, (BLK, BLK), 1)
    scores = jnp.concatenate(
        [
            jnp.where(
                lane < counts[block * list_len + s], scores[:, s * BLK : (s + 1) * BLK], -1e30
            )
            for s in range(list_len)
        ],
        axis=1,
    )
    factor = scale * LOG2E
    highest = jnp.max(scores, axis=-1, keepdims=True) * factor
    expd = jnp.exp2(scores * factor - highest)
    total = jnp.sum(expd, axis=-1, keepdims=True)
    return expd, 1.0 / total, highest + jnp.log2(total)


def forward_kernel(slots, counts, used, *rest, classes, list_len, scale):
    queries_in, velocity_in = rest[:2]
    key_refs, value_refs = rest[2 : 2 + classes], rest[2 + classes : 2 + 2 * classes]
    (
        attn,
        lse,
        squares,
        queries,
        ref_velocity,
        key_pool,
        value_pool,
        sems,
        key_sems,
        value_sems,
    ) = rest[2 + 2 * classes :]
    bring((queries_in, velocity_in), (queries, ref_velocity), sems, 0, True)
    fetch(key_refs, key_pool, key_sems, used, True)
    fetch(value_refs, value_pool, value_sems, used, True)
    rows, cols = queries.shape
    eye = diagonal()
    bring((queries_in, velocity_in), (queries, ref_velocity), sems, 0, False)
    fetch(key_refs, key_pool, key_sems, used, False)
    for block in range(rows // BLK):
        span = slice(block * BLK, (block + 1) * BLK)
        total = jnp.zeros((BLK, 1), jnp.float32)
        for head in range(cols // HD):
            hs = slice(head * HD, (head + 1) * HD)
            keys = listed(key_pool, slots, block, list_len, hs)
            expd, share, log_sum = block_exps(
                queries[span, hs], keys, counts, block, list_len, scale
            )
            if block == 0 and head == 0:
                fetch(value_refs, value_pool, value_sems, used, False)
            values = listed(value_pool, slots, block, list_len, hs)
            out = matmul(expd.astype(jnp.bfloat16), values, NN) * share
            attn[span, hs] = out
            diff = out - ref_velocity[span, hs].astype(jnp.float32)
            total = total + jnp.sum(diff * diff, axis=1, keepdims=True)
            lse[block * 8 : block * 8 + 8, hs] = jnp.broadcast_to(as_row(log_sum, eye), (8, HD))
        squares[block : block + 1, :] = as_row(total, eye)


def upstream_kernel(squares, *rest):
    sources = rest[:4]
    grad, lse, attn, policy_grad, ref_velocity, sems = rest[4:]
    bring(sources, (lse, attn, policy_grad, ref_velocity), sems, 0, True)
    rows, cols = attn.shape
    eye = diagonal()
    weights = []
    for block in range(rows // BLK):
        kl = as_column(squares[block : block + 1, :], eye) / (HEADS * HD)
        weights.append(kl_weight / (1.0 + kl))
    bring(sources, (lse, attn, policy_grad, ref_velocity), sems, 0, False)
    row = lax.broadcasted_iota(jnp.int32, (8, HD), 0)
    tails = []
    for block in range(rows // BLK):
        span = slice(block * BLK, (block + 1) * BLK)
        parts = []
        for head in range(cols // HD):
            hs = slice(head * HD, (head + 1) * HD)
            out = attn[span, hs]
            diff = out - ref_velocity[span, hs].astype(jnp.float32)
            upstream = (policy_grad[span, hs].astype(jnp.float32) + diff * weights[block]).astype(
                jnp.bfloat16
            )
            grad[span, hs] = upstream
            delta = jnp.sum(upstream.astype(jnp.float32) * out, axis=1, keepdims=True)
            tail = jnp.zeros((8, HD), jnp.float32)
            stats = (
                lse[block * 8 : block * 8 + 8, hs],
                jnp.broadcast_to(as_row(delta, eye), (8, HD)),
            )
            for base, left in enumerate(stats):
                for piece in range(3):
                    rounded = left.astype(jnp.bfloat16).astype(jnp.float32)
                    tail = jnp.where(row == base * 3 + piece, rounded, tail)
                    left = left - rounded
            parts.append(tail)
        tails.append(jnp.concatenate(parts, axis=1))
    grad[rows : rows + TAIL, :] = jnp.concatenate(tails, axis=0).astype(jnp.bfloat16)


def query_kernel(slots, counts, used, *rest, classes, list_len, scale):
    sources = rest[:3]
    key_refs, value_refs = rest[3 : 3 + classes], rest[3 + classes : 3 + 2 * classes]
    (
        grad_queries,
        queries,
        grad,
        attn,
        key_pool,
        value_pool,
        sems,
        key_sems,
        value_sems,
    ) = rest[3 + 2 * classes :]
    bring(sources, (queries, grad, attn), sems, 0, True)
    fetch(key_refs, key_pool, key_sems, used, True)
    fetch(value_refs, value_pool, value_sems, used, True)
    rows, cols = queries.shape
    bring(sources, (queries, grad, attn), sems, 0, False)
    fetch(key_refs, key_pool, key_sems, used, False)
    for block in range(rows // BLK):
        span = slice(block * BLK, (block + 1) * BLK)
        for head in range(cols // HD):
            hs = slice(head * HD, (head + 1) * HD)
            keys = listed(key_pool, slots, block, list_len, hs)
            expd, share, _ = block_exps(queries[span, hs], keys, counts, block, list_len, scale)
            if block == 0 and head == 0:
                fetch(value_refs, value_pool, value_sems, used, False)
            values = listed(value_pool, slots, block, list_len, hs)
            upstream = grad[span, hs]
            delta = jnp.sum(upstream.astype(jnp.float32) * attn[span, hs], axis=1, keepdims=True)
            grad_probs = matmul(upstream, values, NT)
            grad_scores = (expd * (grad_probs - delta)).astype(jnp.bfloat16)
            grad_queries[span, hs] = (matmul(grad_scores, keys, NN) * (share * scale)).astype(
                jnp.bfloat16
            )


def naming_kernel(own, valid, *rest, classes, list_len, blocks, rows):
    query_refs = rest[:classes]
    names, lists, sems = rest[classes:]
    targets = [lists.at[pl.ds(position * TAIL, TAIL)] for position in range(classes)]
    sources = [ref.at[pl.ds(rows, TAIL), pl.ds(0, HD)] for ref in query_refs]
    bring(sources, targets, sems, 0, True)
    bring(sources, targets, sems, 0, False)
    names[...] = jnp.zeros_like(names)
    lane = lax.broadcasted_iota(jnp.int32, (TAIL, HD), 1)
    place = lax.broadcasted_iota(jnp.int32, (1, HD), 1)
    for position in range(classes):
        ids = lists[position * TAIL : (position + 1) * TAIL, :].astype(jnp.float32)
        row = jnp.zeros((1, HD), jnp.float32)
        for block in range(blocks):
            mine = (own[0] + block).astype(jnp.float32)
            hit = jnp.where((ids == mine) & (lane < list_len), 1.0, 0.0)
            hit = jnp.max(hit, axis=1, keepdims=True)
            for part in range(blocks):
                row = jnp.where(place == part * blocks + block, hit[part : part + 1], row)
        row = row * valid[position].astype(jnp.float32)
        names[position : position + 1, :] = row.astype(jnp.int32)


def key_kernel(names, counts, *rest, classes, scale):
    keys_in, values_in = rest[:2]
    query_refs, grad_refs = rest[2 : 2 + classes], rest[2 + classes : 2 + 2 * classes]
    (
        grad_keys,
        grad_values,
        keys,
        values,
        query_pool,
        grad_pool,
        acc_k,
        acc_v,
        entries,
        used,
        sems,
        query_sems,
        grad_sems,
    ) = rest[2 + 2 * classes :]
    rows, cols = keys.shape
    blocks = rows // BLK
    height = rows + TAIL
    bring((keys_in, values_in), (keys, values), sems, 0, True)
    for position in range(classes):
        total = names[position, 0]
        for place in range(1, blocks * blocks):
            total = total + names[position, place]
        used[position] = total
    fetch(query_refs, query_pool, query_sems, used, True)
    fetch(grad_refs, grad_pool, grad_sems, used, True)
    lengths = []
    for block in range(blocks):

        def collect(entry, length, block=block):
            hit = names[entry // blocks, (entry % blocks) * blocks + block]
            entries[block, length] = entry
            return length + hit

        length = lax.fori_loop(0, classes * blocks, collect, jnp.int32(0))
        entries[block, length] = 0
        lengths.append(length)
    acc_k[...] = jnp.zeros_like(acc_k)
    acc_v[...] = jnp.zeros_like(acc_v)
    bring((keys_in, values_in), (keys, values), sems, 0, False)
    fetch(query_refs, query_pool, query_sems, used, False)
    fetch(grad_refs, grad_pool, grad_sems, used, False)
    row_in_block = lax.broadcasted_iota(jnp.int32, (BLK, cols), 0)
    for block in range(blocks):
        key_rows = slice(block * BLK, (block + 1) * BLK)
        length = lengths[block]

        def step(chunk, carry, block=block, key_rows=key_rows, length=length):
            places = []
            for lane in range(WIDE):
                index = chunk * WIDE + lane
                live = index < length
                entry = jnp.where(live, entries[block, jnp.minimum(index, length)], 0)
                position, part = entry // blocks, entry % blocks
                places.append(
                    (
                        pl.ds(pl.multiple_of(position * height + part * BLK, 16), BLK),
                        pl.ds(pl.multiple_of(position * height + rows, 16), TAIL),
                        part == 0,
                        jnp.where(live, 0.0, 1e30),
                    )
                )
            for head in range(cols // HD):
                hs = slice(head * HD, (head + 1) * HD)
                query = jnp.concatenate([query_pool[p[0], hs] for p in places], axis=0)
                upstream = jnp.concatenate([grad_pool[p[0], hs] for p in places], axis=0)
                sums, deltas = [], []
                for _, stat_rows, first, extra in places:
                    stats = grad_pool[stat_rows, hs].astype(jnp.float32)
                    stats = jnp.where(first, stats[:8], stats[8:])
                    sums.append(stats[0:1] + stats[1:2] + stats[2:3] + extra)
                    deltas.append(stats[3:4] + stats[4:5] + stats[5:6])
                log_sum = jnp.concatenate(sums, axis=1)
                delta = jnp.concatenate(deltas, axis=1)
                scores = matmul(keys[key_rows, hs], query, NT)
                probs = jnp.exp2(scores * (scale * LOG2E) - log_sum)
                grad_probs = matmul(values[key_rows, hs], upstream, NT)
                grad_scores = (probs * (grad_probs - delta)).astype(jnp.bfloat16)
                acc_v[key_rows, hs] += matmul(probs.astype(jnp.bfloat16), upstream, NN)
                acc_k[key_rows, hs] += matmul(grad_scores, query, NN)
            return carry

        lax.fori_loop(0, (length + WIDE - 1) // WIDE, step, 0)
        valid = row_in_block < counts[block]
        grad_keys[key_rows, :] = jnp.where(valid, acc_k[key_rows, :] * scale, 0.0).astype(
            jnp.bfloat16
        )
        grad_values[key_rows, :] = jnp.where(valid, acc_v[key_rows, :], 0.0).astype(jnp.bfloat16)


SMEM = pl.BlockSpec(memory_space=pltpu.SMEM)
VMEM = pl.BlockSpec(memory_space=pltpu.VMEM)
ANY = pl.BlockSpec(memory_space=pltpu.HBM)


FRAMES = 32
GRID = [(z, y, x) for z in range(2) for y in range(4) for x in range(4)]


def at(z, y, x):
    return z * 16 + y * 4 + x


def flip(bit):
    return [(f, f ^ bit) for f in range(FRAMES)]


def carry_pairs(bit, keep):
    pairs = []
    for f in range(FRAMES):
        if f & bit and f + bit < FRAMES and keep(f, f + bit):
            pairs += [(f, f + bit), (f + bit, f)]
    return pairs


def any_pair(f, g):
    return True


def same_half(f, g):
    return f >> 4 == g >> 4


DIRECT = [
    ("half", "own", flip(16)),
    ("step8", "own", carry_pairs(8, any_pair)),
    ("flip8", "own", flip(8)),
    ("flip4", "own", flip(4)),
    ("step4", "own", carry_pairs(4, same_half)),
    ("flip2", "own", flip(2)),
    ("flip1", "own", flip(1)),
    ("step1", "own", carry_pairs(1, same_half)),
]
RELAYED = [
    (
        "wrap4",
        "half",
        [(at(1, 3, x), at(1, 0, x)) for x in range(4)]
        + [(at(0, 0, x), at(0, 3, x)) for x in range(4)],
    ),
    (
        "wrap2",
        "step8",
        [
            (at(1, 1, 2), at(1, 0, 0)),
            (at(1, 1, 3), at(1, 0, 1)),
            (at(0, 2, 0), at(0, 3, 2)),
            (at(0, 2, 1), at(0, 3, 3)),
        ],
    ),
    ("wrap1", "step8", [(at(1, 1, 3), at(1, 0, 0)), (at(0, 2, 0), at(0, 3, 3))]),
    (
        "row2",
        "turn",
        [(at(z, y, x), at(z, y, x - 2)) for z, y, x in GRID if y > 0 and x > 1]
        + [(at(z, y, x), at(z, y, x + 2)) for z, y, x in GRID if y < 3 and x < 2],
    ),
]
NAMES = ["own"] + [name for name, _, _ in DIRECT + RELAYED]


def turn_takes_flip(f):
    return (f & 3 >= 2) == (f >> 2 & 1 == 1)


def owners():
    held = {"own": list(range(FRAMES))}
    for name, sent, pairs in DIRECT + RELAYED:
        if sent == "turn":
            held["turn"] = [
                held["flip4" if turn_takes_flip(f) else "step4"][f] for f in range(FRAMES)
            ]
        held[name] = [-1] * FRAMES
        for source, target in pairs:
            held[name][target] = held[sent][source]
    table = np.array([held[name] for name in NAMES])
    for f in range(FRAMES):
        got = sorted(o for o in table[:, f] if o >= 0)
        near = {f + s * (1 << level) for level in range(5) for s in (1, -1)} | {f}
        assert got == sorted(o for o in near if 0 <= o < FRAMES)
    return table


def spread(value, turn_flip):
    held = {"own": value}
    for name, sent, pairs in DIRECT + RELAYED:
        if sent == "turn" and "turn" not in held:
            held["turn"] = jnp.where(turn_flip, held["flip4"], held["step4"])
        held[name] = lax.ppermute(held[sent], "frame", pairs)
    return [held[name] for name in NAMES]


def step(queries, keys, values, policy_grad, ref_velocity, key_lists, frame_tokens):
    rows, cols = queries.shape
    blocks = rows // BLK
    list_len = key_lists.shape[1]
    all_blocks = frame_tokens.shape[0]
    scale = 1.0 / math.sqrt(HD)
    assert lax.axis_size("frame") == FRAMES
    me = lax.axis_index("frame")
    classes = len(NAMES)
    f32 = jnp.float32
    turn_flip = (me % 4 >= 2) == (me // 4 % 2 == 1)

    key_pool = spread(keys, turn_flip)
    value_pool = spread(values, turn_flip)

    owner_here = lax.dynamic_slice(
        jnp.asarray(owners().T.astype(np.int32)), (me, 0), (1, classes)
    ).reshape(-1)
    owner = key_lists // blocks
    hits = owner[..., None] == owner_here
    slots = jnp.sum(jnp.where(hits, jnp.arange(classes, dtype=jnp.int32), 0), axis=-1)
    slots = (slots * blocks + key_lists % blocks).reshape(-1)
    used = jnp.any(hits, axis=(0, 1)).astype(jnp.int32)
    valid = (owner_here >= 0).astype(jnp.int32)
    ids = jnp.arange(all_blocks, dtype=jnp.int32)
    counts = jnp.sum(jnp.where(key_lists[..., None] == ids, frame_tokens, 0), axis=-1).reshape(-1)
    own = me * blocks + jnp.arange(blocks, dtype=jnp.int32)
    own_counts = jnp.sum(jnp.where(own[:, None] == ids, frame_tokens, 0), axis=-1)

    lists16 = jnp.pad(
        key_lists.astype(jnp.bfloat16), ((0, TAIL - blocks), (0, cols - list_len))
    )
    tailed = jnp.concatenate([queries, lists16], axis=0)
    tailed, slots, counts, used, valid, own, own_counts = lax.optimization_barrier(
        (tailed, slots, counts, used, valid, own, own_counts)
    )
    query_pool = spread(tailed, turn_flip)

    def shard(dtype=jnp.bfloat16, height=rows):
        return pltpu.VMEM((height, cols), dtype)

    def dma(count):
        return pltpu.SemaphoreType.DMA((count,))

    pools = [shard(height=classes * rows)] * 2
    params = pltpu.CompilerParams(vmem_limit_bytes=20 << 20)
    attn, lse, squares = pl.pallas_call(
        functools.partial(forward_kernel, classes=classes, list_len=list_len, scale=scale),
        out_shape=(
            jax.ShapeDtypeStruct((rows, cols), f32),
            jax.ShapeDtypeStruct((blocks * 8, cols), f32),
            jax.ShapeDtypeStruct((blocks, BLK), f32),
        ),
        in_specs=[SMEM] * 3 + [ANY] * (2 + 2 * classes),
        out_specs=(VMEM, VMEM, VMEM),
        scratch_shapes=[shard(), shard()] + pools + [dma(2), dma(classes), dma(classes)],
        compiler_params=params,
        name="forward",
    )(slots, counts, used, queries, ref_velocity, *key_pool, *value_pool)

    heads = lax.axis_size("head")
    hop = 1
    while hop < heads:
        squares = squares + lax.ppermute(squares, "head", [(i, i ^ hop) for i in range(heads)])
        hop *= 2

    grad = pl.pallas_call(
        upstream_kernel,
        out_shape=jax.ShapeDtypeStruct((rows + TAIL, cols), jnp.bfloat16),
        in_specs=[VMEM] + [ANY] * 4,
        out_specs=VMEM,
        scratch_shapes=[shard(f32, blocks * 8), shard(f32), shard(), shard(), dma(4)],
        compiler_params=params,
        name="upstream",
    )(squares, lse, attn, policy_grad, ref_velocity)

    grad_pool = spread(grad, turn_flip)

    names = pl.pallas_call(
        functools.partial(
            naming_kernel, classes=classes, list_len=list_len, blocks=blocks, rows=rows
        ),
        out_shape=jax.ShapeDtypeStruct((16, HD), jnp.int32),
        in_specs=[SMEM, SMEM] + [ANY] * classes,
        out_specs=VMEM,
        scratch_shapes=[pltpu.VMEM((classes * TAIL, HD), jnp.bfloat16), dma(classes)],
        compiler_params=params,
        name="naming",
    )(own, valid, *query_pool)

    grad_queries = pl.pallas_call(
        functools.partial(query_kernel, classes=classes, list_len=list_len, scale=scale),
        out_shape=jax.ShapeDtypeStruct((rows, cols), jnp.bfloat16),
        in_specs=[SMEM] * 3 + [ANY] * (3 + 2 * classes),
        out_specs=VMEM,
        scratch_shapes=[shard(), shard(height=rows + TAIL), shard(f32)]
        + pools
        + [dma(3), dma(classes), dma(classes)],
        compiler_params=params,
        name="grad_queries",
    )(slots, counts, used, queries, grad, attn, *key_pool, *value_pool)

    grad_keys, grad_values = pl.pallas_call(
        functools.partial(key_kernel, classes=classes, scale=scale),
        out_shape=(
            jax.ShapeDtypeStruct((rows, cols), jnp.bfloat16),
            jax.ShapeDtypeStruct((rows, cols), jnp.bfloat16),
        ),
        in_specs=[SMEM, SMEM] + [ANY] * (2 + 2 * classes),
        out_specs=(VMEM, VMEM),
        scratch_shapes=[shard(), shard()]
        + [shard(height=classes * (rows + TAIL))] * 2
        + [
            shard(f32),
            shard(f32),
            pltpu.SMEM((blocks, 32), jnp.int32),
            pltpu.SMEM((classes,), jnp.int32),
            dma(2),
            dma(classes),
            dma(classes),
        ],
        compiler_params=params,
        name="grad_keys_values",
    )(names, own_counts, keys, values, *query_pool, *grad_pool)
    return grad_queries, grad_keys, grad_values


def solution(mesh):
    in_specs = (
        P("frame", "head"),
        P("frame", "head"),
        P("frame", "head"),
        P("frame", "head"),
        P("frame", "head"),
        P("frame", None),
        P(),
    )
    out_specs = (P("frame", "head"), P("frame", "head"), P("frame", "head"))
    return jax.shard_map(step, mesh=mesh, in_specs=in_specs, out_specs=out_specs, check_vma=False)
```

```python
import functools
import math

import jax
import jax.numpy as jnp
import numpy as np
from jax import lax
from jax.experimental import pallas as pl
from jax.experimental.pallas import tpu as pltpu
from jax.sharding import PartitionSpec as P

HEADS = 40
HD = 128
BLK = 128
TAIL = 16

kl_weight = 1.0
LOG2E = 1.4426950408889634


WIDE = 4

NT = (((1,), (1,)), ((), ()))
NN = (((1,), (0,)), ((), ()))


def matmul(left, right, dims):
    return lax.dot_general(left, right, dims, preferred_element_type=jnp.float32)


def diagonal():
    return lax.broadcasted_iota(jnp.int32, (BLK, BLK), 0) == lax.broadcasted_iota(
        jnp.int32, (BLK, BLK), 1
    )


def as_row(column, eye):
    return jnp.sum(jnp.where(eye, column, 0.0), axis=0, keepdims=True)


def as_column(row, eye):
    return jnp.sum(jnp.where(eye, row, 0.0), axis=1, keepdims=True)


def bring(sources, targets, sems, first, start):
    for position, (source, target) in enumerate(zip(sources, targets)):
        copy = pltpu.make_async_copy(source, target, sems.at[first + position])
        if start:
            copy.start()
        else:
            copy.wait()


def fetch(sources, pool, sems, used, start):
    height = pool.shape[0] // len(sources)
    for position, source in enumerate(sources):

        @pl.when(used[position] != 0)
        def _():
            copy = pltpu.make_async_copy(
                source, pool.at[pl.ds(position * height, height)], sems.at[position]
            )
            if start:
                copy.start()
            else:
                copy.wait()


def listed(pool, slots, block, list_len, cols):
    return jnp.concatenate(
        [
            pool[pl.ds(pl.multiple_of(slots[block * list_len + s] * BLK, BLK), BLK), cols]
            for s in range(list_len)
        ],
        axis=0,
    )


def block_exps(query, key_block, counts, block, list_len, scale):
    scores = matmul(query, key_block, NT)
    lane = lax.broadcasted_iota(jnp.int32, (BLK, BLK), 1)
    scores = jnp.concatenate(
        [
            jnp.where(
                lane < counts[block * list_len + s], scores[:, s * BLK : (s + 1) * BLK], -1e30
            )
            for s in range(list_len)
        ],
        axis=1,
    )
    factor = scale * LOG2E
    highest = jnp.max(scores, axis=-1, keepdims=True) * factor
    expd = jnp.exp2(scores * factor - highest)
    total = jnp.sum(expd, axis=-1, keepdims=True)
    return expd, 1.0 / total, highest + jnp.log2(total)


def forward_kernel(slots, counts, used, *rest, classes, list_len, scale):
    queries_in, velocity_in = rest[:2]
    key_refs, value_refs = rest[2 : 2 + classes], rest[2 + classes : 2 + 2 * classes]
    (
        attn,
        lse,
        squares,
        queries,
        ref_velocity,
        key_pool,
        value_pool,
        sems,
        key_sems,
        value_sems,
    ) = rest[2 + 2 * classes :]
    bring((queries_in, velocity_in), (queries, ref_velocity), sems, 0, True)
    fetch(key_refs, key_pool, key_sems, used, True)
    fetch(value_refs, value_pool, value_sems, used, True)
    rows, cols = queries.shape
    eye = diagonal()
    bring((queries_in, velocity_in), (queries, ref_velocity), sems, 0, False)
    fetch(key_refs, key_pool, key_sems, used, False)
    for block in range(rows // BLK):
        span = slice(block * BLK, (block + 1) * BLK)
        total = jnp.zeros((BLK, 1), jnp.float32)
        for head in range(cols // HD):
            hs = slice(head * HD, (head + 1) * HD)
            keys = listed(key_pool, slots, block, list_len, hs)
            expd, share, log_sum = block_exps(
                queries[span, hs], keys, counts, block, list_len, scale
            )
            if block == 0 and head == 0:
                fetch(value_refs, value_pool, value_sems, used, False)
            values = listed(value_pool, slots, block, list_len, hs)
            out = matmul(expd.astype(jnp.bfloat16), values, NN) * share
            attn[span, hs] = out
            diff = out - ref_velocity[span, hs].astype(jnp.float32)
            total = total + jnp.sum(diff * diff, axis=1, keepdims=True)
            lse[block * 8 : block * 8 + 8, hs] = jnp.broadcast_to(as_row(log_sum, eye), (8, HD))
        squares[block : block + 1, :] = as_row(total, eye)


def upstream_kernel(squares, *rest):
    sources = rest[:4]
    grad, lse, attn, policy_grad, ref_velocity, sems = rest[4:]
    bring(sources, (lse, attn, policy_grad, ref_velocity), sems, 0, True)
    rows, cols = attn.shape
    eye = diagonal()
    weights = []
    for block in range(rows // BLK):
        kl = as_column(squares[block : block + 1, :], eye) / (HEADS * HD)
        weights.append(kl_weight / (1.0 + kl))
    bring(sources, (lse, attn, policy_grad, ref_velocity), sems, 0, False)
    row = lax.broadcasted_iota(jnp.int32, (8, HD), 0)
    tails = []
    for block in range(rows // BLK):
        span = slice(block * BLK, (block + 1) * BLK)
        parts = []
        for head in range(cols // HD):
            hs = slice(head * HD, (head + 1) * HD)
            out = attn[span, hs]
            diff = out - ref_velocity[span, hs].astype(jnp.float32)
            upstream = (policy_grad[span, hs].astype(jnp.float32) + diff * weights[block]).astype(
                jnp.bfloat16
            )
            grad[span, hs] = upstream
            delta = jnp.sum(upstream.astype(jnp.float32) * out, axis=1, keepdims=True)
            tail = jnp.zeros((8, HD), jnp.float32)
            stats = (
                lse[block * 8 : block * 8 + 8, hs],
                jnp.broadcast_to(as_row(delta, eye), (8, HD)),
            )
            for base, left in enumerate(stats):
                for piece in range(3):
                    rounded = left.astype(jnp.bfloat16).astype(jnp.float32)
                    tail = jnp.where(row == base * 3 + piece, rounded, tail)
                    left = left - rounded
            parts.append(tail)
        tails.append(jnp.concatenate(parts, axis=1))
    grad[rows : rows + TAIL, :] = jnp.concatenate(tails, axis=0).astype(jnp.bfloat16)


def query_kernel(slots, counts, used, *rest, classes, list_len, scale):
    sources = rest[:3]
    key_refs, value_refs = rest[3 : 3 + classes], rest[3 + classes : 3 + 2 * classes]
    (
        grad_queries,
        queries,
        grad,
        attn,
        key_pool,
        value_pool,
        sems,
        key_sems,
        value_sems,
    ) = rest[3 + 2 * classes :]
    bring(sources, (queries, grad, attn), sems, 0, True)
    fetch(key_refs, key_pool, key_sems, used, True)
    fetch(value_refs, value_pool, value_sems, used, True)
    rows, cols = queries.shape
    bring(sources, (queries, grad, attn), sems, 0, False)
    fetch(key_refs, key_pool, key_sems, used, False)
    for block in range(rows // BLK):
        span = slice(block * BLK, (block + 1) * BLK)
        for head in range(cols // HD):
            hs = slice(head * HD, (head + 1) * HD)
            keys = listed(key_pool, slots, block, list_len, hs)
            expd, share, _ = block_exps(queries[span, hs], keys, counts, block, list_len, scale)
            if block == 0 and head == 0:
                fetch(value_refs, value_pool, value_sems, used, False)
            values = listed(value_pool, slots, block, list_len, hs)
            upstream = grad[span, hs]
            delta = jnp.sum(upstream.astype(jnp.float32) * attn[span, hs], axis=1, keepdims=True)
            grad_probs = matmul(upstream, values, NT)
            grad_scores = (expd * (grad_probs - delta)).astype(jnp.bfloat16)
            grad_queries[span, hs] = (matmul(grad_scores, keys, NN) * (share * scale)).astype(
                jnp.bfloat16
            )


def naming_kernel(own, valid, *rest, classes, list_len, blocks, rows):
    query_refs = rest[:classes]
    names, lists, sems = rest[classes:]
    targets = [lists.at[pl.ds(position * TAIL, TAIL)] for position in range(classes)]
    sources = [ref.at[pl.ds(rows, TAIL), pl.ds(0, HD)] for ref in query_refs]
    bring(sources, targets, sems, 0, True)
    bring(sources, targets, sems, 0, False)
    names[...] = jnp.zeros_like(names)
    lane = lax.broadcasted_iota(jnp.int32, (TAIL, HD), 1)
    place = lax.broadcasted_iota(jnp.int32, (1, HD), 1)
    for position in range(classes):
        ids = lists[position * TAIL : (position + 1) * TAIL, :].astype(jnp.float32)
        row = jnp.zeros((1, HD), jnp.float32)
        for block in range(blocks):
            mine = (own[0] + block).astype(jnp.float32)
            hit = jnp.where((ids == mine) & (lane < list_len), 1.0, 0.0)
            hit = jnp.max(hit, axis=1, keepdims=True)
            for part in range(blocks):
                row = jnp.where(place == part * blocks + block, hit[part : part + 1], row)
        row = row * valid[position].astype(jnp.float32)
        names[position : position + 1, :] = row.astype(jnp.int32)


def key_kernel(names, counts, *rest, classes, scale):
    keys_in, values_in = rest[:2]
    query_refs, grad_refs = rest[2 : 2 + classes], rest[2 + classes : 2 + 2 * classes]
    (
        grad_keys,
        grad_values,
        keys,
        values,
        query_pool,
        grad_pool,
        acc_k,
        acc_v,
        entries,
        used,
        sems,
        query_sems,
        grad_sems,
    ) = rest[2 + 2 * classes :]
    rows, cols = keys.shape
    blocks = rows // BLK
    height = rows + TAIL
    bring((keys_in, values_in), (keys, values), sems, 0, True)
    for position in range(classes):
        total = names[position, 0]
        for place in range(1, blocks * blocks):
            total = total + names[position, place]
        used[position] = total
    fetch(query_refs, query_pool, query_sems, used, True)
    fetch(grad_refs, grad_pool, grad_sems, used, True)
    lengths = []
    for block in range(blocks):

        def collect(entry, length, block=block):
            hit = names[entry // blocks, (entry % blocks) * blocks + block]
            entries[block, length] = entry
            return length + hit

        length = lax.fori_loop(0, classes * blocks, collect, jnp.int32(0))
        entries[block, length] = 0
        lengths.append(length)
    acc_k[...] = jnp.zeros_like(acc_k)
    acc_v[...] = jnp.zeros_like(acc_v)
    bring((keys_in, values_in), (keys, values), sems, 0, False)
    fetch(query_refs, query_pool, query_sems, used, False)
    fetch(grad_refs, grad_pool, grad_sems, used, False)
    row_in_block = lax.broadcasted_iota(jnp.int32, (BLK, cols), 0)
    for block in range(blocks):
        key_rows = slice(block * BLK, (block + 1) * BLK)
        length = lengths[block]

        def step(chunk, carry, block=block, key_rows=key_rows, length=length):
            places = []
            for lane in range(WIDE):
                index = chunk * WIDE + lane
                live = index < length
                entry = jnp.where(live, entries[block, jnp.minimum(index, length)], 0)
                position, part = entry // blocks, entry % blocks
                places.append(
                    (
                        pl.ds(pl.multiple_of(position * height + part * BLK, 16), BLK),
                        pl.ds(pl.multiple_of(position * height + rows, 16), TAIL),
                        part == 0,
                        jnp.where(live, 0.0, 1e30),
                    )
                )
            for head in range(cols // HD):
                hs = slice(head * HD, (head + 1) * HD)
                query = jnp.concatenate([query_pool[p[0], hs] for p in places], axis=0)
                upstream = jnp.concatenate([grad_pool[p[0], hs] for p in places], axis=0)
                sums, deltas = [], []
                for _, stat_rows, first, extra in places:
                    stats = grad_pool[stat_rows, hs].astype(jnp.float32)
                    stats = jnp.where(first, stats[:8], stats[8:])
                    sums.append(stats[0:1] + stats[1:2] + stats[2:3] + extra)
                    deltas.append(stats[3:4] + stats[4:5] + stats[5:6])
                log_sum = jnp.concatenate(sums, axis=1)
                delta = jnp.concatenate(deltas, axis=1)
                scores = matmul(keys[key_rows, hs], query, NT)
                probs = jnp.exp2(scores * (scale * LOG2E) - log_sum)
                grad_probs = matmul(values[key_rows, hs], upstream, NT)
                grad_scores = (probs * (grad_probs - delta)).astype(jnp.bfloat16)
                acc_v[key_rows, hs] += matmul(probs.astype(jnp.bfloat16), upstream, NN)
                acc_k[key_rows, hs] += matmul(grad_scores, query, NN)
            return carry

        lax.fori_loop(0, (length + WIDE - 1) // WIDE, step, 0)
        valid = row_in_block < counts[block]
        grad_keys[key_rows, :] = jnp.where(valid, acc_k[key_rows, :] * scale, 0.0).astype(
            jnp.bfloat16
        )
        grad_values[key_rows, :] = jnp.where(valid, acc_v[key_rows, :], 0.0).astype(jnp.bfloat16)


SMEM = pl.BlockSpec(memory_space=pltpu.SMEM)
VMEM = pl.BlockSpec(memory_space=pltpu.VMEM)
ANY = pl.BlockSpec(memory_space=pltpu.HBM)


FRAMES = 32
GRID = [(z, y, x) for z in range(2) for y in range(4) for x in range(4)]


def at(z, y, x):
    return z * 16 + y * 4 + x


def flip(bit):
    return [(f, f ^ bit) for f in range(FRAMES)]


def carry_pairs(bit, keep):
    pairs = []
    for f in range(FRAMES):
        if f & bit and f + bit < FRAMES and keep(f, f + bit):
            pairs += [(f, f + bit), (f + bit, f)]
    return pairs


def any_pair(f, g):
    return True


def same_half(f, g):
    return f >> 4 == g >> 4


DIRECT = [
    ("half", "own", flip(16)),
    ("step8", "own", carry_pairs(8, any_pair)),
    ("flip8", "own", flip(8)),
    ("flip4", "own", flip(4)),
    ("step4", "own", carry_pairs(4, same_half)),
    ("flip2", "own", flip(2)),
    ("flip1", "own", flip(1)),
    ("step1", "own", carry_pairs(1, same_half)),
]
RELAYED = [
    (
        "wrap4",
        "half",
        [(at(1, 3, x), at(1, 0, x)) for x in range(4)]
        + [(at(0, 0, x), at(0, 3, x)) for x in range(4)],
    ),
    (
        "wrap2",
        "step8",
        [
            (at(1, 1, 2), at(1, 0, 0)),
            (at(1, 1, 3), at(1, 0, 1)),
            (at(0, 2, 0), at(0, 3, 2)),
            (at(0, 2, 1), at(0, 3, 3)),
        ],
    ),
    ("wrap1", "step8", [(at(1, 1, 3), at(1, 0, 0)), (at(0, 2, 0), at(0, 3, 3))]),
    (
        "row2",
        "turn",
        [(at(z, y, x), at(z, y, x - 2)) for z, y, x in GRID if y > 0 and x > 1]
        + [(at(z, y, x), at(z, y, x + 2)) for z, y, x in GRID if y < 3 and x < 2],
    ),
]
NAMES = ["own"] + [name for name, _, _ in DIRECT + RELAYED]
LIGHT = [flow for flow in DIRECT if flow[0] != "step8"] + [
    (
        "step8",
        "half",
        [(at(1, y, x), at(1, y - 2, x)) for y in (2, 3) for x in range(4)]
        + [(at(0, y, x), at(0, y + 2, x)) for y in (0, 1) for x in range(4)],
    ),
    RELAYED[0],
    (
        "wrap2",
        "half",
        [
            (at(1, 3, 2), at(1, 0, 0)),
            (at(1, 3, 3), at(1, 0, 1)),
            (at(0, 0, 0), at(0, 3, 2)),
            (at(0, 0, 1), at(0, 3, 3)),
        ],
    ),
    ("wrap1", "half", [(at(1, 3, 3), at(1, 0, 0)), (at(0, 0, 0), at(0, 3, 3))]),
    RELAYED[3],
]


LIGHT_FLOWS = "q"


def turn_takes_flip(f):
    return (f & 3 >= 2) == (f >> 2 & 1 == 1)


def owners(flows):
    held = {"own": list(range(FRAMES))}
    for name, sent, pairs in flows:
        if sent == "turn":
            held["turn"] = [
                held["flip4" if turn_takes_flip(f) else "step4"][f] for f in range(FRAMES)
            ]
        held[name] = [-1] * FRAMES
        for source, target in pairs:
            held[name][target] = held[sent][source]
    table = np.array([held[name] for name in NAMES])
    for f in range(FRAMES):
        got = sorted(o for o in table[:, f] if o >= 0)
        near = {f + s * (1 << level) for level in range(5) for s in (1, -1)} | {f}
        assert got == sorted(o for o in near if 0 <= o < FRAMES)
    return table


def spread(value, turn_flip, prefix):
    held = {"own": value}
    for name, sent, pairs in LIGHT if prefix in LIGHT_FLOWS else DIRECT + RELAYED:
        if sent == "turn" and "turn" not in held:
            held["turn"] = jnp.where(turn_flip, held["flip4"], held["step4"])
        held[name] = lax.ppermute(held[sent], "frame", pairs)
    return [held[name] for name in NAMES]


def step(queries, keys, values, policy_grad, ref_velocity, key_lists, frame_tokens):
    rows, cols = queries.shape
    blocks = rows // BLK
    list_len = key_lists.shape[1]
    all_blocks = frame_tokens.shape[0]
    scale = 1.0 / math.sqrt(HD)
    assert lax.axis_size("frame") == FRAMES
    me = lax.axis_index("frame")
    classes = len(NAMES)
    f32 = jnp.float32
    turn_flip = (me % 4 >= 2) == (me // 4 % 2 == 1)

    key_pool = spread(keys, turn_flip, "k")
    value_pool = spread(values, turn_flip, "v")

    table = owners(DIRECT + RELAYED)
    assert (table == owners(LIGHT)).all()
    owner_here = lax.dynamic_slice(
        jnp.asarray(table.T.astype(np.int32)), (me, 0), (1, classes)
    ).reshape(-1)
    owner = key_lists // blocks
    hits = owner[..., None] == owner_here
    slots = jnp.sum(jnp.where(hits, jnp.arange(classes, dtype=jnp.int32), 0), axis=-1)
    slots = (slots * blocks + key_lists % blocks).reshape(-1)
    used = jnp.any(hits, axis=(0, 1)).astype(jnp.int32)
    valid = (owner_here >= 0).astype(jnp.int32)
    ids = jnp.arange(all_blocks, dtype=jnp.int32)
    counts = jnp.sum(jnp.where(key_lists[..., None] == ids, frame_tokens, 0), axis=-1).reshape(-1)
    own = me * blocks + jnp.arange(blocks, dtype=jnp.int32)
    own_counts = jnp.sum(jnp.where(own[:, None] == ids, frame_tokens, 0), axis=-1)

    lists16 = jnp.pad(
        key_lists.astype(jnp.bfloat16), ((0, TAIL - blocks), (0, cols - list_len))
    )
    tailed = jnp.concatenate([queries, lists16], axis=0)
    tailed, slots, counts, used, valid, own, own_counts = lax.optimization_barrier(
        (tailed, slots, counts, used, valid, own, own_counts)
    )
    query_pool = spread(tailed, turn_flip, "q")

    def shard(dtype=jnp.bfloat16, height=rows):
        return pltpu.VMEM((height, cols), dtype)

    def dma(count):
        return pltpu.SemaphoreType.DMA((count,))

    pools = [shard(height=classes * rows)] * 2
    params = pltpu.CompilerParams(vmem_limit_bytes=20 << 20)
    attn, lse, squares = pl.pallas_call(
        functools.partial(forward_kernel, classes=classes, list_len=list_len, scale=scale),
        out_shape=(
            jax.ShapeDtypeStruct((rows, cols), f32),
            jax.ShapeDtypeStruct((blocks * 8, cols), f32),
            jax.ShapeDtypeStruct((blocks, BLK), f32),
        ),
        in_specs=[SMEM] * 3 + [ANY] * (2 + 2 * classes),
        out_specs=(VMEM, VMEM, VMEM),
        scratch_shapes=[shard(), shard()] + pools + [dma(2), dma(classes), dma(classes)],
        compiler_params=params,
        name="forward",
    )(slots, counts, used, queries, ref_velocity, *key_pool, *value_pool)

    heads = lax.axis_size("head")
    hop = 1
    while hop < heads:
        squares = squares + lax.ppermute(squares, "head", [(i, i ^ hop) for i in range(heads)])
        hop *= 2

    grad = pl.pallas_call(
        upstream_kernel,
        out_shape=jax.ShapeDtypeStruct((rows + TAIL, cols), jnp.bfloat16),
        in_specs=[VMEM] + [ANY] * 4,
        out_specs=VMEM,
        scratch_shapes=[shard(f32, blocks * 8), shard(f32), shard(), shard(), dma(4)],
        compiler_params=params,
        name="upstream",
    )(squares, lse, attn, policy_grad, ref_velocity)

    grad_pool = spread(grad, turn_flip, "d")

    names = pl.pallas_call(
        functools.partial(
            naming_kernel, classes=classes, list_len=list_len, blocks=blocks, rows=rows
        ),
        out_shape=jax.ShapeDtypeStruct((16, HD), jnp.int32),
        in_specs=[SMEM, SMEM] + [ANY] * classes,
        out_specs=VMEM,
        scratch_shapes=[pltpu.VMEM((classes * TAIL, HD), jnp.bfloat16), dma(classes)],
        compiler_params=params,
        name="naming",
    )(own, valid, *query_pool)

    grad_queries = pl.pallas_call(
        functools.partial(query_kernel, classes=classes, list_len=list_len, scale=scale),
        out_shape=jax.ShapeDtypeStruct((rows, cols), jnp.bfloat16),
        in_specs=[SMEM] * 3 + [ANY] * (3 + 2 * classes),
        out_specs=VMEM,
        scratch_shapes=[shard(), shard(height=rows + TAIL), shard(f32)]
        + pools
        + [dma(3), dma(classes), dma(classes)],
        compiler_params=params,
        name="grad_queries",
    )(slots, counts, used, queries, grad, attn, *key_pool, *value_pool)

    grad_keys, grad_values = pl.pallas_call(
        functools.partial(key_kernel, classes=classes, scale=scale),
        out_shape=(
            jax.ShapeDtypeStruct((rows, cols), jnp.bfloat16),
            jax.ShapeDtypeStruct((rows, cols), jnp.bfloat16),
        ),
        in_specs=[SMEM, SMEM] + [ANY] * (2 + 2 * classes),
        out_specs=(VMEM, VMEM),
        scratch_shapes=[shard(), shard()]
        + [shard(height=classes * (rows + TAIL))] * 2
        + [
            shard(f32),
            shard(f32),
            pltpu.SMEM((blocks, 32), jnp.int32),
            pltpu.SMEM((classes,), jnp.int32),
            dma(2),
            dma(classes),
            dma(classes),
        ],
        compiler_params=params,
        name="grad_keys_values",
    )(names, own_counts, keys, values, *query_pool, *grad_pool)
    return grad_queries, grad_keys, grad_values


def solution(mesh):
    in_specs = (
        P("frame", "head"),
        P("frame", "head"),
        P("frame", "head"),
        P("frame", "head"),
        P("frame", "head"),
        P("frame", None),
        P(),
    )
    out_specs = (P("frame", "head"), P("frame", "head"), P("frame", "head"))
    return jax.shard_map(step, mesh=mesh, in_specs=in_specs, out_specs=out_specs, check_vma=False)
```

```python
import functools
import math

import jax
import jax.numpy as jnp
import numpy as np
from jax import lax
from jax.experimental import pallas as pl
from jax.experimental.pallas import tpu as pltpu
from jax.sharding import PartitionSpec as P

HEADS = 40
HD = 128
BLK = 128
TAIL = 16

kl_weight = 1.0
LOG2E = 1.4426950408889634


WIDE = 4

NT = (((1,), (1,)), ((), ()))
NN = (((1,), (0,)), ((), ()))


def matmul(left, right, dims):
    return lax.dot_general(left, right, dims, preferred_element_type=jnp.float32)


def diagonal():
    return lax.broadcasted_iota(jnp.int32, (BLK, BLK), 0) == lax.broadcasted_iota(
        jnp.int32, (BLK, BLK), 1
    )


def as_row(column, eye):
    return jnp.sum(jnp.where(eye, column, 0.0), axis=0, keepdims=True)


def as_column(row, eye):
    return jnp.sum(jnp.where(eye, row, 0.0), axis=1, keepdims=True)


def bring(sources, targets, sems, first, start):
    for position, (source, target) in enumerate(zip(sources, targets)):
        copy = pltpu.make_async_copy(source, target, sems.at[first + position])
        if start:
            copy.start()
        else:
            copy.wait()


def fetch(sources, pool, sems, used, start):
    height = pool.shape[0] // len(sources)
    for position, source in enumerate(sources):

        @pl.when(used[position] != 0)
        def _():
            copy = pltpu.make_async_copy(
                source, pool.at[pl.ds(position * height, height)], sems.at[position]
            )
            if start:
                copy.start()
            else:
                copy.wait()


def listed(pool, slots, block, list_len, cols):
    return jnp.concatenate(
        [
            pool[pl.ds(pl.multiple_of(slots[block * list_len + s] * BLK, BLK), BLK), cols]
            for s in range(list_len)
        ],
        axis=0,
    )


def block_exps(query, key_block, counts, block, list_len, scale):
    scores = matmul(query, key_block, NT)
    lane = lax.broadcasted_iota(jnp.int32, (BLK, BLK), 1)
    scores = jnp.concatenate(
        [
            jnp.where(
                lane < counts[block * list_len + s], scores[:, s * BLK : (s + 1) * BLK], -1e30
            )
            for s in range(list_len)
        ],
        axis=1,
    )
    factor = scale * LOG2E
    highest = jnp.max(scores, axis=-1, keepdims=True) * factor
    expd = jnp.exp2(scores * factor - highest)
    total = jnp.sum(expd, axis=-1, keepdims=True)
    return expd, 1.0 / total, highest + jnp.log2(total)


def forward_kernel(slots, counts, used, *rest, classes, list_len, scale):
    queries_in, velocity_in = rest[:2]
    key_refs, value_refs = rest[2 : 2 + classes], rest[2 + classes : 2 + 2 * classes]
    (
        attn,
        lse,
        squares,
        queries,
        ref_velocity,
        key_pool,
        value_pool,
        sems,
        key_sems,
        value_sems,
    ) = rest[2 + 2 * classes :]
    bring((queries_in, velocity_in), (queries, ref_velocity), sems, 0, True)
    fetch(key_refs, key_pool, key_sems, used, True)
    fetch(value_refs, value_pool, value_sems, used, True)
    rows, cols = queries.shape
    eye = diagonal()
    bring((queries_in, velocity_in), (queries, ref_velocity), sems, 0, False)
    fetch(key_refs, key_pool, key_sems, used, False)
    for block in range(rows // BLK):
        span = slice(block * BLK, (block + 1) * BLK)
        total = jnp.zeros((BLK, 1), jnp.float32)
        for head in range(cols // HD):
            hs = slice(head * HD, (head + 1) * HD)
            keys = listed(key_pool, slots, block, list_len, hs)
            expd, share, log_sum = block_exps(
                queries[span, hs], keys, counts, block, list_len, scale
            )
            if block == 0 and head == 0:
                fetch(value_refs, value_pool, value_sems, used, False)
            values = listed(value_pool, slots, block, list_len, hs)
            out = matmul(expd.astype(jnp.bfloat16), values, NN) * share
            attn[span, hs] = out
            diff = out - ref_velocity[span, hs].astype(jnp.float32)
            total = total + jnp.sum(diff * diff, axis=1, keepdims=True)
            lse[block * 8 : block * 8 + 8, hs] = jnp.broadcast_to(as_row(log_sum, eye), (8, HD))
        squares[block : block + 1, :] = as_row(total, eye)


def upstream_kernel(squares, *rest):
    sources = rest[:4]
    grad, lse, attn, policy_grad, ref_velocity, sems = rest[4:]
    bring(sources, (lse, attn, policy_grad, ref_velocity), sems, 0, True)
    rows, cols = attn.shape
    eye = diagonal()
    weights = []
    for block in range(rows // BLK):
        kl = as_column(squares[block : block + 1, :], eye) / (HEADS * HD)
        weights.append(kl_weight / (1.0 + kl))
    bring(sources, (lse, attn, policy_grad, ref_velocity), sems, 0, False)
    row = lax.broadcasted_iota(jnp.int32, (8, HD), 0)
    tails = []
    for block in range(rows // BLK):
        span = slice(block * BLK, (block + 1) * BLK)
        parts = []
        for head in range(cols // HD):
            hs = slice(head * HD, (head + 1) * HD)
            out = attn[span, hs]
            diff = out - ref_velocity[span, hs].astype(jnp.float32)
            upstream = (policy_grad[span, hs].astype(jnp.float32) + diff * weights[block]).astype(
                jnp.bfloat16
            )
            grad[span, hs] = upstream
            delta = jnp.sum(upstream.astype(jnp.float32) * out, axis=1, keepdims=True)
            tail = jnp.zeros((8, HD), jnp.float32)
            stats = (
                lse[block * 8 : block * 8 + 8, hs],
                jnp.broadcast_to(as_row(delta, eye), (8, HD)),
            )
            for base, left in enumerate(stats):
                for piece in range(3):
                    rounded = left.astype(jnp.bfloat16).astype(jnp.float32)
                    tail = jnp.where(row == base * 3 + piece, rounded, tail)
                    left = left - rounded
            parts.append(tail)
        tails.append(jnp.concatenate(parts, axis=1))
    grad[rows : rows + TAIL, :] = jnp.concatenate(tails, axis=0).astype(jnp.bfloat16)


def query_kernel(slots, counts, used, *rest, classes, list_len, scale):
    sources = rest[:3]
    key_refs, value_refs = rest[3 : 3 + classes], rest[3 + classes : 3 + 2 * classes]
    (
        grad_queries,
        queries,
        grad,
        attn,
        key_pool,
        value_pool,
        sems,
        key_sems,
        value_sems,
    ) = rest[3 + 2 * classes :]
    bring(sources, (queries, grad, attn), sems, 0, True)
    fetch(key_refs, key_pool, key_sems, used, True)
    fetch(value_refs, value_pool, value_sems, used, True)
    rows, cols = queries.shape
    bring(sources, (queries, grad, attn), sems, 0, False)
    fetch(key_refs, key_pool, key_sems, used, False)
    for block in range(rows // BLK):
        span = slice(block * BLK, (block + 1) * BLK)
        for head in range(cols // HD):
            hs = slice(head * HD, (head + 1) * HD)
            keys = listed(key_pool, slots, block, list_len, hs)
            expd, share, _ = block_exps(queries[span, hs], keys, counts, block, list_len, scale)
            if block == 0 and head == 0:
                fetch(value_refs, value_pool, value_sems, used, False)
            values = listed(value_pool, slots, block, list_len, hs)
            upstream = grad[span, hs]
            delta = jnp.sum(upstream.astype(jnp.float32) * attn[span, hs], axis=1, keepdims=True)
            grad_probs = matmul(upstream, values, NT)
            grad_scores = (expd * (grad_probs - delta)).astype(jnp.bfloat16)
            grad_queries[span, hs] = (matmul(grad_scores, keys, NN) * (share * scale)).astype(
                jnp.bfloat16
            )


def naming_kernel(own, valid, *rest, classes, list_len, blocks, rows):
    query_refs = rest[:classes]
    names, lists, sems = rest[classes:]
    targets = [lists.at[pl.ds(position * TAIL, TAIL)] for position in range(classes)]
    sources = [ref.at[pl.ds(rows, TAIL), pl.ds(0, HD)] for ref in query_refs]
    bring(sources, targets, sems, 0, True)
    bring(sources, targets, sems, 0, False)
    names[...] = jnp.zeros_like(names)
    lane = lax.broadcasted_iota(jnp.int32, (TAIL, HD), 1)
    place = lax.broadcasted_iota(jnp.int32, (1, HD), 1)
    for position in range(classes):
        ids = lists[position * TAIL : (position + 1) * TAIL, :].astype(jnp.float32)
        row = jnp.zeros((1, HD), jnp.float32)
        for block in range(blocks):
            mine = (own[0] + block).astype(jnp.float32)
            hit = jnp.where((ids == mine) & (lane < list_len), 1.0, 0.0)
            hit = jnp.max(hit, axis=1, keepdims=True)
            for part in range(blocks):
                row = jnp.where(place == part * blocks + block, hit[part : part + 1], row)
        row = row * valid[position].astype(jnp.float32)
        names[position : position + 1, :] = row.astype(jnp.int32)


def key_kernel(names, counts, *rest, base, classes, scale):
    sources = rest[: 2 if base == 0 else 4]
    rest = rest[len(sources) :]
    query_refs, grad_refs, rest = rest[:classes], rest[classes : 2 * classes], rest[2 * classes :]
    if base == 0:
        (acc_k, acc_v), rest = rest[:2], rest[2:]
    else:
        (grad_keys, grad_values, acc_k, acc_v), rest = rest[:4], rest[4:]
    (
        keys,
        values,
        query_pool,
        grad_pool,
        entries,
        used,
        sems,
        query_sems,
        grad_sems,
    ) = rest
    targets = (keys, values) if base == 0 else (keys, values, acc_k, acc_v)
    rows, cols = keys.shape
    blocks = rows // BLK
    height = rows + TAIL
    bring(sources, targets, sems, 0, True)
    for position in range(classes):
        total = names[base + position, 0]
        for place in range(1, blocks * blocks):
            total = total + names[base + position, place]
        used[position] = total
    fetch(query_refs, query_pool, query_sems, used, True)
    fetch(grad_refs, grad_pool, grad_sems, used, True)
    lengths = []
    for block in range(blocks):

        def collect(entry, length, block=block):
            hit = names[base + entry // blocks, (entry % blocks) * blocks + block]
            entries[block, length] = entry
            return length + hit

        length = lax.fori_loop(0, classes * blocks, collect, jnp.int32(0))
        lengths.append(length)
    if base == 0:
        acc_k[...] = jnp.zeros_like(acc_k)
        acc_v[...] = jnp.zeros_like(acc_v)
    bring(sources, targets, sems, 0, False)
    fetch(query_refs, query_pool, query_sems, used, False)
    fetch(grad_refs, grad_pool, grad_sems, used, False)
    row_in_block = lax.broadcasted_iota(jnp.int32, (BLK, cols), 0)
    for block in range(blocks):
        key_rows = slice(block * BLK, (block + 1) * BLK)
        length = lengths[block]

        def step(chunk, carry, block=block, key_rows=key_rows, length=length):
            places = []
            for lane in range(WIDE):
                index = chunk * WIDE + lane
                live = index < length
                entry = entries[block, jnp.minimum(index, length - 1)]
                position, part = entry // blocks, entry % blocks
                places.append(
                    (
                        pl.ds(pl.multiple_of(position * height + part * BLK, 16), BLK),
                        pl.ds(pl.multiple_of(position * height + rows, 16), TAIL),
                        part == 0,
                        jnp.where(live, 0.0, 1e30),
                    )
                )
            for head in range(cols // HD):
                hs = slice(head * HD, (head + 1) * HD)
                query = jnp.concatenate([query_pool[p[0], hs] for p in places], axis=0)
                upstream = jnp.concatenate([grad_pool[p[0], hs] for p in places], axis=0)
                sums, deltas = [], []
                for _, stat_rows, first, extra in places:
                    stats = grad_pool[stat_rows, hs].astype(jnp.float32)
                    stats = jnp.where(first, stats[:8], stats[8:])
                    sums.append(stats[0:1] + stats[1:2] + stats[2:3] + extra)
                    deltas.append(stats[3:4] + stats[4:5] + stats[5:6])
                log_sum = jnp.concatenate(sums, axis=1)
                delta = jnp.concatenate(deltas, axis=1)
                scores = matmul(keys[key_rows, hs], query, NT)
                probs = jnp.exp2(scores * (scale * LOG2E) - log_sum)
                grad_probs = matmul(values[key_rows, hs], upstream, NT)
                grad_scores = (probs * (grad_probs - delta)).astype(jnp.bfloat16)
                acc_v[key_rows, hs] += matmul(probs.astype(jnp.bfloat16), upstream, NN)
                acc_k[key_rows, hs] += matmul(grad_scores, query, NN)
            return carry

        lax.fori_loop(0, (length + WIDE - 1) // WIDE, step, 0)
        if base == 0:
            continue
        valid = row_in_block < counts[block]
        grad_keys[key_rows, :] = jnp.where(valid, acc_k[key_rows, :] * scale, 0.0).astype(
            jnp.bfloat16
        )
        grad_values[key_rows, :] = jnp.where(valid, acc_v[key_rows, :], 0.0).astype(jnp.bfloat16)


SMEM = pl.BlockSpec(memory_space=pltpu.SMEM)
VMEM = pl.BlockSpec(memory_space=pltpu.VMEM)
ANY = pl.BlockSpec(memory_space=pltpu.HBM)


FRAMES = 32
GRID = [(z, y, x) for z in range(2) for y in range(4) for x in range(4)]


def at(z, y, x):
    return z * 16 + y * 4 + x


def flip(bit):
    return [(f, f ^ bit) for f in range(FRAMES)]


def carry_pairs(bit, keep):
    pairs = []
    for f in range(FRAMES):
        if f & bit and f + bit < FRAMES and keep(f, f + bit):
            pairs += [(f, f + bit), (f + bit, f)]
    return pairs


def any_pair(f, g):
    return True


def same_half(f, g):
    return f >> 4 == g >> 4


DIRECT = [
    ("half", "own", flip(16)),
    ("flip8", "own", flip(8)),
    ("flip4", "own", flip(4)),
    ("step4", "own", carry_pairs(4, same_half)),
    ("flip2", "own", flip(2)),
    ("flip1", "own", flip(1)),
    ("step1", "own", carry_pairs(1, same_half)),
    ("step8", "own", carry_pairs(8, any_pair)),
]
RELAYED = [
    (
        "wrap4",
        "half",
        [(at(1, 3, x), at(1, 0, x)) for x in range(4)]
        + [(at(0, 0, x), at(0, 3, x)) for x in range(4)],
    ),
    (
        "wrap2",
        "step8",
        [
            (at(1, 1, 2), at(1, 0, 0)),
            (at(1, 1, 3), at(1, 0, 1)),
            (at(0, 2, 0), at(0, 3, 2)),
            (at(0, 2, 1), at(0, 3, 3)),
        ],
    ),
    ("wrap1", "step8", [(at(1, 1, 3), at(1, 0, 0)), (at(0, 2, 0), at(0, 3, 3))]),
    (
        "row2",
        "turn",
        [(at(z, y, x), at(z, y, x - 2)) for z, y, x in GRID if y > 0 and x > 1]
        + [(at(z, y, x), at(z, y, x + 2)) for z, y, x in GRID if y < 3 and x < 2],
    ),
]
EARLY = len(DIRECT) + 1
NAMES = ["own"] + [name for name, _, _ in DIRECT + RELAYED]
LIGHT = [flow for flow in DIRECT if flow[0] != "step8"] + [
    (
        "step8",
        "half",
        [(at(1, y, x), at(1, y - 2, x)) for y in (2, 3) for x in range(4)]
        + [(at(0, y, x), at(0, y + 2, x)) for y in (0, 1) for x in range(4)],
    ),
    RELAYED[0],
    (
        "wrap2",
        "half",
        [
            (at(1, 3, 2), at(1, 0, 0)),
            (at(1, 3, 3), at(1, 0, 1)),
            (at(0, 0, 0), at(0, 3, 2)),
            (at(0, 0, 1), at(0, 3, 3)),
        ],
    ),
    ("wrap1", "half", [(at(1, 3, 3), at(1, 0, 0)), (at(0, 0, 0), at(0, 3, 3))]),
    RELAYED[3],
]


LIGHT_FLOWS = "q"


def turn_takes_flip(f):
    return (f & 3 >= 2) == (f >> 2 & 1 == 1)


def owners(flows):
    held = {"own": list(range(FRAMES))}
    for name, sent, pairs in flows:
        if sent == "turn":
            held["turn"] = [
                held["flip4" if turn_takes_flip(f) else "step4"][f] for f in range(FRAMES)
            ]
        held[name] = [-1] * FRAMES
        for source, target in pairs:
            held[name][target] = held[sent][source]
    table = np.array([held[name] for name in NAMES])
    for f in range(FRAMES):
        got = sorted(o for o in table[:, f] if o >= 0)
        near = {f + s * (1 << level) for level in range(5) for s in (1, -1)} | {f}
        assert got == sorted(o for o in near if 0 <= o < FRAMES)
    return table


def spread(value, turn_flip, prefix):
    held = {"own": value}
    for name, sent, pairs in LIGHT if prefix in LIGHT_FLOWS else DIRECT + RELAYED:
        if sent == "turn" and "turn" not in held:
            held["turn"] = jnp.where(turn_flip, held["flip4"], held["step4"])
        held[name] = lax.ppermute(held[sent], "frame", pairs)
    return [held[name] for name in NAMES]


def step(queries, keys, values, policy_grad, ref_velocity, key_lists, frame_tokens):
    rows, cols = queries.shape
    blocks = rows // BLK
    list_len = key_lists.shape[1]
    all_blocks = frame_tokens.shape[0]
    scale = 1.0 / math.sqrt(HD)
    assert lax.axis_size("frame") == FRAMES
    me = lax.axis_index("frame")
    classes = len(NAMES)
    f32 = jnp.float32
    turn_flip = (me % 4 >= 2) == (me // 4 % 2 == 1)

    key_pool = spread(keys, turn_flip, "k")
    value_pool = spread(values, turn_flip, "v")

    table = owners(DIRECT + RELAYED)
    assert (table == owners(LIGHT)).all()
    owner_here = lax.dynamic_slice(
        jnp.asarray(table.T.astype(np.int32)), (me, 0), (1, classes)
    ).reshape(-1)
    owner = key_lists // blocks
    hits = owner[..., None] == owner_here
    slots = jnp.sum(jnp.where(hits, jnp.arange(classes, dtype=jnp.int32), 0), axis=-1)
    slots = (slots * blocks + key_lists % blocks).reshape(-1)
    used = jnp.any(hits, axis=(0, 1)).astype(jnp.int32)
    valid = (owner_here >= 0).astype(jnp.int32)
    ids = jnp.arange(all_blocks, dtype=jnp.int32)
    counts = jnp.sum(jnp.where(key_lists[..., None] == ids, frame_tokens, 0), axis=-1).reshape(-1)
    own = me * blocks + jnp.arange(blocks, dtype=jnp.int32)
    own_counts = jnp.sum(jnp.where(own[:, None] == ids, frame_tokens, 0), axis=-1)

    lists16 = jnp.pad(
        key_lists.astype(jnp.bfloat16), ((0, TAIL - blocks), (0, cols - list_len))
    )
    tailed = jnp.concatenate([queries, lists16], axis=0)
    tailed, slots, counts, used, valid, own, own_counts = lax.optimization_barrier(
        (tailed, slots, counts, used, valid, own, own_counts)
    )
    query_pool = spread(tailed, turn_flip, "q")

    def shard(dtype=jnp.bfloat16, height=rows):
        return pltpu.VMEM((height, cols), dtype)

    def dma(count):
        return pltpu.SemaphoreType.DMA((count,))

    pools = [shard(height=classes * rows)] * 2
    params = pltpu.CompilerParams(vmem_limit_bytes=20 << 20)
    attn, lse, squares = pl.pallas_call(
        functools.partial(forward_kernel, classes=classes, list_len=list_len, scale=scale),
        out_shape=(
            jax.ShapeDtypeStruct((rows, cols), f32),
            jax.ShapeDtypeStruct((blocks * 8, cols), f32),
            jax.ShapeDtypeStruct((blocks, BLK), f32),
        ),
        in_specs=[SMEM] * 3 + [ANY] * (2 + 2 * classes),
        out_specs=(VMEM, VMEM, VMEM),
        scratch_shapes=[shard(), shard()] + pools + [dma(2), dma(classes), dma(classes)],
        compiler_params=params,
        name="forward",
    )(slots, counts, used, queries, ref_velocity, *key_pool, *value_pool)

    heads = lax.axis_size("head")
    hop = 1
    while hop < heads:
        squares = squares + lax.ppermute(squares, "head", [(i, i ^ hop) for i in range(heads)])
        hop *= 2

    grad = pl.pallas_call(
        upstream_kernel,
        out_shape=jax.ShapeDtypeStruct((rows + TAIL, cols), jnp.bfloat16),
        in_specs=[VMEM] + [ANY] * 4,
        out_specs=VMEM,
        scratch_shapes=[shard(f32, blocks * 8), shard(f32), shard(), shard(), dma(4)],
        compiler_params=params,
        name="upstream",
    )(squares, lse, attn, policy_grad, ref_velocity)

    grad_pool = spread(grad, turn_flip, "d")

    names = pl.pallas_call(
        functools.partial(
            naming_kernel, classes=classes, list_len=list_len, blocks=blocks, rows=rows
        ),
        out_shape=jax.ShapeDtypeStruct((16, HD), jnp.int32),
        in_specs=[SMEM, SMEM] + [ANY] * classes,
        out_specs=VMEM,
        scratch_shapes=[pltpu.VMEM((classes * TAIL, HD), jnp.bfloat16), dma(classes)],
        compiler_params=params,
        name="naming",
    )(own, valid, *query_pool)

    grad_queries = pl.pallas_call(
        functools.partial(query_kernel, classes=classes, list_len=list_len, scale=scale),
        out_shape=jax.ShapeDtypeStruct((rows, cols), jnp.bfloat16),
        in_specs=[SMEM] * 3 + [ANY] * (3 + 2 * classes),
        out_specs=VMEM,
        scratch_shapes=[shard(), shard(height=rows + TAIL), shard(f32)]
        + pools
        + [dma(3), dma(classes), dma(classes)],
        compiler_params=params,
        name="grad_queries",
    )(slots, counts, used, queries, grad, attn, *key_pool, *value_pool)

    def key_call(base, count, outs):
        inputs = 2 if base == 0 else 4
        return pl.pallas_call(
            functools.partial(key_kernel, base=base, classes=count, scale=scale),
            out_shape=(outs, outs),
            in_specs=[SMEM, SMEM] + [ANY] * (inputs + 2 * count),
            out_specs=(VMEM, VMEM),
            scratch_shapes=([] if base == 0 else [shard(f32), shard(f32)])
            + [shard(), shard()]
            + [shard(height=count * (rows + TAIL))] * 2
            + [
                pltpu.SMEM((blocks, 32), jnp.int32),
                pltpu.SMEM((count,), jnp.int32),
                dma(inputs),
                dma(count),
                dma(count),
            ],
            compiler_params=params,
        )

    sums = key_call(0, EARLY, jax.ShapeDtypeStruct((rows, cols), f32))(names, own_counts, keys, values, *query_pool[:EARLY], *grad_pool[:EARLY])
    grad_keys, grad_values = key_call(
        EARLY, classes - EARLY, jax.ShapeDtypeStruct((rows, cols), jnp.bfloat16)
    )(names, own_counts, keys, values, *sums, *query_pool[EARLY:], *grad_pool[EARLY:])
    return grad_queries, grad_keys, grad_values


def solution(mesh):
    in_specs = (
        P("frame", "head"),
        P("frame", "head"),
        P("frame", "head"),
        P("frame", "head"),
        P("frame", "head"),
        P("frame", None),
        P(),
    )
    out_specs = (P("frame", "head"), P("frame", "head"), P("frame", "head"))
    return jax.shard_map(step, mesh=mesh, in_specs=in_specs, out_specs=out_specs, check_vma=False)
```
